32 devices in a mesh: space: 8 (over y, x, core), chan: 4 (over z).
Axes of the slice: x: 2, y: 2, z: 4, core: 2. Of those that a mesh axis runs over, the one named last changes fastest.
Arguments:
- feats: bfloat16 [96, 8, 8, 128], P('chan', 'space'), may hold values from -6 to 6
- grads: bfloat16 [96, 8, 8, 128], P('chan', 'space'), may hold values from -6 to 6
- mask: int32 [8, 8, 128], P('space', None, 'chan'), may hold values 0 or 1
- w_first: bfloat16 [27, 96, 96], replicated, may hold values from -0.125 to 0.125
- w_second: bfloat16 [27, 96, 96], replicated, may hold values from -0.125 to 0.125
Outputs:
- grad_feats: bfloat16 [96, 8, 8, 128], P('chan', 'space')
- grad_first: float32 [27, 96, 96], P(None, None, 'chan')
- grad_second: float32 [27, 96, 96], P(None, None, 'chan')
The draws below stay inside these ranges and needn't reach their ends.
All inputs are finite; a program needn't handle non-finite values. No bound on the sum of `mask` on one device may be relied on, other than what follows from the above.
Results may differ from the reference program's by a relative error of at most 0.02.
Values may be sent and summed in bfloat16 or wider, within the bound.
A program may use at most 64 MiB of HBM per device.

```python
import jax
import jax.numpy as jnp

C = 96
TAPS = 27
SY = 8
NX = 8
NZ = 128


def with_ends(drawn, key, low, top_value):
    dims = drawn.shape
    spot = [jax.random.randint(jax.random.fold_in(key, axis), (), 0, dims[axis]) for axis in range(len(dims))]
    drawn = drawn.at[tuple(spot)].set(low)
    longest = dims.index(max(dims))
    spot[longest] = (spot[longest] + 1) % dims[longest]
    return drawn.at[tuple(spot)].set(top_value)


def with_spikes(values, rng, source, target, parts, factor):
    def block_of(position):
        return (jnp.arange(values.shape[position]) // (values.shape[position] // parts)).reshape((-1,) + (1,) * (values.ndim - 1 - position))

    first = jax.random.permutation(rng, parts)[block_of(target)]
    second = (block_of(target) + parts // 2) % parts
    return jnp.where((block_of(source) == first) | (block_of(source) == second), factor * values, values)


def levels(stream_key, dims, split, least, high):
    loudness, own = 1.0, jax.random.fold_in(stream_key, 6)
    for position, parts in split:
        draws = jnp.exp(jax.random.uniform(jax.random.fold_in(own, position), (parts,), jnp.float32, least / len(split), high / len(split)))
        loudness = loudness * jnp.repeat(draws, dims[position] // parts).reshape([-1 if axis == position else 1 for axis in range(len(dims))])
    return loudness


def normal_values(rng, dims, deviation, bound, split=(), dtype=jnp.bfloat16):
    drawn = jax.random.normal(rng, dims, jnp.float32) * deviation
    if len(split) > 0:
        drawn = levels(rng, dims, split, -0.22, 0.18) * drawn
    return jnp.clip(drawn, min=-bound, max=bound).astype(dtype)


def noise_with(stream_key, shape, spread, reach, pieces, heavy, held_as=jnp.bfloat16):
    drawn = spread * jax.random.normal(stream_key, shape, jnp.float32)
    if pieces:
        drawn = drawn * levels(stream_key, shape, pieces, -0.22, 0.18)
    return jnp.clip(with_spikes(drawn, jax.random.fold_in(stream_key, 3), *heavy), -reach, reach).astype(held_as)


def setup_inputs(seed: int = 0) -> dict:
    splits = jax.random.split(jax.random.key(seed), 6)
    return {
        "feats": normal_values(splits[0], (C, NX, SY, NZ), 1.0, 6.0, ((0, 4), (1, 8))),
        "grads": noise_with(splits[1], (C, NX, SY, NZ), 1.0, 6.0, ((0, 4), (1, 8)), (1, 0, 8, 2.0)),
        "mask": with_ends((jax.random.randint(splits[2], (NX, SY, NZ), 0, 4) < 3).astype(jnp.int32), jax.random.fold_in(splits[2], 1), 0, 1),
        "w_first": normal_values(splits[3], (TAPS, C, C), (TAPS * C) ** -0.5, 0.125),
        "w_second": normal_values(splits[4], (TAPS, C, C), (TAPS * C) ** -0.5, 0.125),
    }


offset_table = [(a, b, c) for a in (-1, 0, 1) for b in (-1, 0, 1) for c in (-1, 0, 1)]

def padded_field(field):
    return jnp.pad(field, ((0, 0), (1, 1), (1, 1), (1, 1)))

def shifted(padded, a, b, c):
    channels, xs, ys, zs = padded.shape
    piece = padded[:, 1 + a:xs - 1 + a, 1 + b:ys - 1 + b, 1 + c:zs - 1 + c]
    return piece.reshape(channels, -1)

def reference(feats, grads, mask, w_first, w_second):
    channels, xs, ys, zs = feats.shape
    cells = xs * ys * zs
    weight_mask = mask.astype(jnp.float32).reshape(1, cells)
    padded_x = padded_field(feats)
    pre = jnp.zeros((channels, cells), jnp.float32)
    for k, (a, b, c) in enumerate(offset_table):
        pre = pre + jnp.dot(w_first[k].T, shifted(padded_x, a, b, c), preferred_element_type=jnp.float32)
    pre = pre * weight_mask
    sigm = jax.nn.sigmoid(pre)
    active = (pre * sigm).astype(jnp.bfloat16)
    masked = grads * mask.astype(jnp.bfloat16)[None]
    padded_g = padded_field(masked)
    back = jnp.zeros((channels, cells), jnp.float32)
    seconds = []
    for k, (a, b, c) in enumerate(offset_table):
        moved = shifted(padded_g, -a, -b, -c)
        back = back + jnp.dot(w_second[k], moved, preferred_element_type=jnp.float32)
        seconds.append(jnp.dot(active, moved.T, preferred_element_type=jnp.float32))
    slope = sigm * (1.0 + pre * (1.0 - sigm))
    grad_pre = (back * slope * weight_mask).astype(jnp.bfloat16)
    padded_h = padded_field(grad_pre.reshape(channels, xs, ys, zs))
    grad_in = jnp.zeros((channels, cells), jnp.float32)
    firsts = []
    for k, (a, b, c) in enumerate(offset_table):
        grad_in = grad_in + jnp.dot(w_first[k], shifted(padded_h, -a, -b, -c), preferred_element_type=jnp.float32)
        firsts.append(jnp.dot(shifted(padded_x, a, b, c), grad_pre.T, preferred_element_type=jnp.float32))
    grad_feats = (grad_in * weight_mask).astype(jnp.bfloat16).reshape(channels, xs, ys, zs)
    scale = 1.0 / jnp.sqrt(jnp.float32(cells))
    grad_first = jnp.stack(firsts) * scale
    grad_second = jnp.stack(seconds) * scale
    return (grad_feats, grad_first, grad_second)
```

```python
import functools

import jax
import jax.numpy as jnp
from jax import lax
from jax.experimental import pallas as pl
from jax.experimental.pallas import tpu as pltpu
from jax.sharding import PartitionSpec as P

MESH = pl.DeviceIdType.MESH
F32 = jnp.float32
BF16 = jnp.bfloat16


def dot_nn(left, right):
    return jnp.dot(left, right, preferred_element_type=F32)


def dot_nt(left, right):
    return lax.dot_general(left, right, (((1,), (1,)), ((), ())), preferred_element_type=F32)


def one_hot(rows, cols, target):
    r = lax.broadcasted_iota(jnp.int32, (rows, cols), 0)
    q = lax.broadcasted_iota(jnp.int32, (rows, cols), 1)
    return jnp.where(target(r, q), 1.0, 0.0).astype(BF16)


def lane_shift(x, s):
    if s == 0:
        return x
    n = x.shape[1]
    z = lax.broadcasted_iota(jnp.int32, x.shape, 1)
    if s == 1:
        return jnp.where(z < n - 1, pltpu.roll(x, n - 1, 1), 0.0)
    return jnp.where(z > 0, pltpu.roll(x, 1, 1), 0.0)


def spread(out_ref, rows_of, cb, ys, zs):
    for y in range(ys):
        row = rows_of(y)
        for c in (-1, 0, 1):
            moved = lane_shift(row, -c)
            for b in (-1, 0, 1):
                j = 3 * (b + 1) + (c + 1)
                if 0 <= y + b < ys:
                    out_ref[j * cb : (j + 1) * cb, (y + b) * zs : (y + b + 1) * zs] = moved
    edge = jnp.zeros((3 * cb, zs), F32)
    out_ref[0 : 3 * cb, (ys - 1) * zs : ys * zs] = edge
    out_ref[6 * cb : 9 * cb, 0:zs] = edge


def kernel(
    n, nz, cb, ys, zs, scale, sp, ch_name,
    f_hbm, g_hbm, mask_hbm, w1_hbm, w2_hbm,
    gf_ref, g1_ref, g2_ref,
    w1_ref, w2_ref, mi_ref, ws, B, MK, MX, X, WA, WB, WCF, WC, TR, AC, SL, GPF, GP, SH, SM, TA, PA, PR,
    R32, RB, RP, CS, GF,
    zss, zrs, hss, hrs, mss, mrs, mhs, mhr, pss, prs, r1s, r1r, r2s, r2r, r3s, r3r,
):
    s = lax.axis_index(sp)
    me = lax.axis_index(ch_name)
    full = w1_ref.shape[1]
    cells = ys * zs
    kb = X.shape[2]
    kc = GP.shape[0]
    cp = -(-cb // 16) * 16
    mz = mi_ref.shape[1]
    rows = 27 * cb
    half = RB.shape[2]
    ry = max(1, 256 // zs)
    nch = n // 2
    tiles = zs // 128
    core = lax.rem(s, 2)
    chip = lax.div(s, 2)
    partner = s + 1 - 2 * core
    left, right = s > 0, s < n - 1

    def copy(src, dst, ssem, rsem, ds, dc):
        return pltpu.make_async_remote_copy(
            src_ref=src, dst_ref=dst, send_sem=ssem, recv_sem=rsem,
            device_id=(ds, dc), device_id_type=MESH,
        )

    load_m = pltpu.make_async_copy(mask_hbm, mi_ref, ws.at[2])
    load_f = pltpu.make_async_copy(f_hbm, B.at[0, 1, me], ws.at[3])
    load_g = pltpu.make_async_copy(g_hbm, B.at[1, 1, me], ws.at[4])
    load1 = pltpu.make_async_copy(w1_hbm, w1_ref, ws.at[0])
    load2 = pltpu.make_async_copy(w2_hbm, w2_ref, ws.at[1])
    load_m.start()
    load_f.start()
    load_g.start()
    load1.start()
    load2.start()
    barrier = pltpu.get_barrier_semaphore()

    @pl.loop(1, nz)
    def _(i):
        pl.semaphore_signal(barrier, inc=1, device_id=(s, lax.rem(me + i, nz)), device_id_type=MESH)

    @pl.loop(1, n)
    def _(i):
        pl.semaphore_signal(barrier, inc=1, device_id=(lax.rem(s + i, n), me), device_id_type=MESH)

    for kind in range(2):
        X[kind] = jnp.zeros(X.shape[1:], BF16)
    GP[...] = jnp.zeros(GP.shape, BF16)
    WCF[...] = jnp.zeros(WCF.shape, F32)
    tail = R32.shape[1] - rows
    if tail:
        for g in range(2):
            R32[g, rows:, :] = jnp.zeros((tail, full), F32)
    load_m.wait()
    place = one_hot(mz, zs, lambda r, q: q == r + mz * me)
    MK[me] = dot_nn(mi_ref[...].astype(F32).astype(BF16), place)
    load_f.wait()
    load_g.wait()
    pl.semaphore_wait(barrier, n + nz - 2)

    def z_copy(i, buf, ssem, rsem):
        return copy(buf, buf, ssem.at[i], rsem.at[i], s, lax.rem(me + i, nz))

    order = sorted(range(1, nz), key=lambda i: min(i, nz - i))
    for i in order:
        z_copy(i, MK.at[me], mss, mrs).start()
    for kind in range(2):
        for i in order:
            z_copy(i, B.at[kind, 1, me], zss.at[kind], zrs.at[kind]).start()

    def halo(kind, c, start):
        src = B.at[kind, 1, c]

        @pl.when(right)
        def _():
            d = copy(src, B.at[kind, 0, c], hss.at[kind, 0, c], hrs.at[kind, 0, c], s + 1, me)
            d.start() if start else d.wait_send()

        @pl.when(left)
        def _():
            d = copy(src, B.at[kind, 2, c], hss.at[kind, 1, c], hrs.at[kind, 1, c], s - 1, me)
            d.start() if start else d.wait_send()

    halo(1, me, True)
    halo(0, me, True)

    load1.wait()
    load2.wait()
    pick = one_hot(cb, full, lambda r, q: q == r + cb * me)
    same = one_hot(full, full, lambda r, q: q == r)
    widen = one_hot(kb, full, lambda r, q: r == (q // cb) * cp + lax.rem(q, cb))
    for a in range(3):
        for b in range(3):
            lanes = slice((3 * a + b) * kb, (3 * a + b + 1) * kb)
            for c in range(3):
                k = 9 * a + 3 * b + c
                w1 = w1_ref[k]
                wide = dot_nn(widen, w1).astype(BF16)
                WA[c * full : (c + 1) * full, lanes] = dot_nt(same, wide).astype(BF16)
                WB[c * full : (c + 1) * full, lanes] = dot_nt(w2_ref[k], widen).astype(BF16)
                WCF[(3 * a + c) * cb : (3 * a + c + 1) * cb, b * kc : b * kc + full] = dot_nn(pick, w1)
    WC[...] = WCF[...].astype(BF16)

    for i in order:
        c = lax.rem(me + nz - i, nz)
        copy(MK.at[c], MK.at[c], mss.at[i], mrs.at[i], s, c).wait_recv()
    own_mask = MK[0]
    for c in range(1, nz):
        own_mask = own_mask + MK[c]
    MX[1] = own_mask

    @pl.when(right)
    def _():
        copy(MX.at[1], MX.at[0], mhs.at[0], mhr.at[0], s + 1, me).start()

    @pl.when(left)
    def _():
        copy(MX.at[1], MX.at[2], mhs.at[1], mhr.at[1], s - 1, me).start()

    def native(kind, slab, c):
        x = B[kind, slab, c].astype(F32)
        if kind:
            x = (x.reshape(cb, ys, zs) * MX[slab][None]).reshape(cb * ys, zs)
        return x

    def put(ref, x):
        for q in range(tiles):
            ref[q] = x[:, q * 128 : (q + 1) * 128]

    def take(ref, y):
        return jnp.concatenate([ref[q, pl.ds(y, cb, stride=ys), :] for q in range(tiles)], axis=1)

    def whole(ref):
        return jnp.concatenate([ref[q] for q in range(tiles)], axis=1)

    def relayout(kind, slab, c, t):
        put(TR.at[t], native(kind, slab, c))
        at = pl.ds(pl.multiple_of(c * cp, 16), cb)
        for y in range(ys):
            X[kind, slab, at, (1 + y) * zs : (2 + y) * zs] = take(TR.at[t], y).astype(BF16)

    def arrive(kind):
        for i in order:
            c = lax.rem(me + nz - i, nz)
            copy(B.at[kind, 1, c], B.at[kind, 1, c], zss.at[kind, i], zrs.at[kind, i], s, c).wait_recv()
            halo(kind, c, True)
            relayout(kind, 1, c, i)

    def arrive_halo(kind):
        for side, slab, there in ((0, 0, left), (1, 2, right)):

            @pl.when(there)
            def _():
                for c in range(nz):
                    copy(B.at[kind, slab, c], B.at[kind, slab, c], hss.at[kind, side, c], hrs.at[kind, side, c], s, me).wait_recv()
                    relayout(kind, slab, c, c)

    def conv(kind, W, step, direction):
        for y0 in range(0, ys, ry):
            parts = []
            for a in range(3):
                slab = a if direction == 1 else 2 - a
                for b in range(3):
                    y = y0 + 1 + direction * (b - 1)
                    parts.append(X[kind, slab, :, y * zs : (y + ry) * zs])
            res = dot_nn(W[...], jnp.concatenate(parts, axis=0))
            for r in range(ry):
                acc = None
                for c in range(3):
                    piece = lane_shift(res[c * full : (c + 1) * full, r * zs : (r + 1) * zs], direction * (c - 1))
                    acc = piece if acc is None else acc + piece
                step(y0 + r, acc)

    relayout(0, 1, me, 0)
    arrive(0)
    relayout(1, 1, me, 0)
    arrive(1)

    def spread_masked(slab):
        put(TR.at[0], native(1, slab, me))
        spread(SH, lambda y: take(TR.at[0], y), cb, ys, zs)
        SM[2 - slab] = SH[...].astype(BF16)

    spread_masked(1)
    for side, slab, there in ((0, 0, left), (1, 2, right)):

        @pl.when(there)
        def _():
            copy(MX.at[slab], MX.at[slab], mhs.at[side], mhr.at[side], s, me).wait_recv()
            copy(B.at[1, slab, me], B.at[1, slab, me], hss.at[1, side, me], hrs.at[1, side, me], s, me).wait_recv()
            spread_masked(slab)
            relayout(1, slab, me, 0)

        @pl.when(jnp.logical_not(there))
        def _():
            SM[2 - slab] = jnp.zeros(SM.shape[1:], BF16)

    arrive_halo(0)

    def pre_step(y, acc):
        at = slice(y * zs, (y + 1) * zs)
        m = MX[1, y : y + 1, :]
        pre = acc * m
        sig = jax.nn.sigmoid(pre)
        AC[:, at] = (pre * sig).astype(BF16)
        SL[:, at] = sig * (1.0 + pre * (1.0 - sig)) * m

    conv(0, WA, pre_step, 1)

    def pair_start(g):
        RB[g] = R32[g].astype(BF16).reshape(RB.shape[1:])
        copy(RB.at[g, 1 - core], RP.at[g], r1s.at[g], r1r.at[g], partner, me).start()

    def chips(g, start):
        @pl.loop(1, nch)
        def _(i):
            to = lax.rem(chip + i, nch)
            d = copy(CS.at[g, chip], CS.at[g, chip], r2s.at[g, i], r2r.at[g, i], 2 * to + core, me)
            d.start() if start else d.wait_send()

    def chip_sum(g):
        copy(RP.at[g], RP.at[g], r1s.at[g], r1r.at[g], partner, me).wait_recv()
        own = R32[g, pl.ds(pl.multiple_of(core * half, 8), half), :]
        CS[g, chip] = (own + RP[g].astype(F32)).astype(BF16)
        chips(g, True)

    def total(g):
        @pl.loop(1, nch)
        def _(i):
            j = lax.rem(chip + nch - i, nch)
            copy(CS.at[g, j], CS.at[g, j], r2s.at[g, i], r2r.at[g, i], s, me).wait_recv()

        acc = CS[g, 0].astype(F32)
        for j in range(1, nch):
            acc = acc + CS[g, j].astype(F32)
        GF[g, core] = acc
        copy(GF.at[g, core], GF.at[g, core], r3s.at[g], r3r.at[g], partner, me).start()

    def finish(g, out_ref):
        other = GF.at[g, 1 - core]
        copy(other, other, r3s.at[g], r3r.at[g], partner, me).wait_recv()
        out_ref[...] = GF[g].reshape(out_ref.shape)

    for a in range(3):
        R32[1, 9 * cb * a : 9 * cb * (a + 1), :] = dot_nt(SM[a], AC[...]) * scale
    pair_start(1)

    def wait_halo_grads():
        for side, slab, there in ((0, 0, left), (1, 2, right)):

            @pl.when(there)
            def _():
                @pl.loop(1, nz)
                def _(i):
                    c = lax.rem(me + i, nz)
                    copy(B.at[1, slab, c], B.at[1, slab, c], hss.at[1, side, c], hrs.at[1, side, c], s, me).wait_recv()
                    relayout(1, slab, c, i)

    chip_sum(1)
    wait_halo_grads()

    def back_step(y, acc):
        gp = acc * SL[:, y * zs : (y + 1) * zs]
        GPF[:, y * zs : (y + 1) * zs] = gp
        GP[0:full, (1 + y) * zs : (2 + y) * zs] = gp.astype(BF16)

    conv(1, WB, back_step, -1)

    own_rows = pl.ds(pl.multiple_of(me * cb, 8), cb)
    spread(SH, lambda y: GPF[own_rows, y * zs : (y + 1) * zs], cb, ys, zs)
    moved = SH[...].astype(BF16)
    narrow = one_hot(full, kb, lambda r, q: q == (r // cb) * cp + lax.rem(r, cb))
    for a in range(3):
        wide = (dot_nt(moved, X[0, a, :, zs : zs + cells]) * scale).astype(BF16)
        R32[0, 9 * cb * a : 9 * cb * (a + 1), :] = dot_nt(wide, narrow)
    pair_start(0)

    for y0 in range(0, ys, ry):
        parts = []
        for b in range(3):
            y = y0 + 1 - (b - 1)
            parts.append(GP[:, y * zs : (y + ry) * zs])
        res = dot_nn(WC[...], jnp.concatenate(parts, axis=0))
        for a in range(3):
            for r in range(ry):
                acc = None
                for c in range(3):
                    j = 3 * a + c
                    piece = lane_shift(res[j * cb : (j + 1) * cb, r * zs : (r + 1) * zs], -(c - 1))
                    acc = piece if acc is None else acc + piece
                for q in range(tiles):
                    TA[a, q, pl.ds(y0 + r, cb, stride=ys), :] = acc[:, q * 128 : (q + 1) * 128]
    PA[0] = whole(TA.at[0]).astype(BF16)
    PA[1] = whole(TA.at[2]).astype(BF16)

    @pl.when(right)
    def _():
        copy(PA.at[1], PR.at[0], pss.at[0], prs.at[0], s + 1, me).start()

    @pl.when(left)
    def _():
        copy(PA.at[0], PR.at[1], pss.at[1], prs.at[1], s - 1, me).start()

    chip_sum(0)
    total(1)

    for side, there in ((0, left), (1, right)):

        @pl.when(there)
        def _():
            copy(PR.at[side], PR.at[side], pss.at[side], prs.at[side], s, me).wait_recv()
            put(TA.at[1], whole(TA.at[1]) + PR[side].astype(F32))

    gf = whole(TA.at[1]).reshape(cb, ys, zs) * MX[1][None]
    gf_ref[...] = gf.reshape(cb * ys, zs).astype(BF16)

    finish(1, g2_ref)
    total(0)
    finish(0, g1_ref)

    for i in order:
        z_copy(i, MK.at[me], mss, mrs).wait_send()
        for kind in range(2):
            z_copy(i, B.at[kind, 1, me], zss.at[kind], zrs.at[kind]).wait_send()

    @pl.when(right)
    def _():
        copy(MX.at[1], MX.at[0], mhs.at[0], mhr.at[0], s + 1, me).wait_send()
        copy(PA.at[1], PR.at[0], pss.at[0], prs.at[0], s + 1, me).wait_send()

    @pl.when(left)
    def _():
        copy(MX.at[1], MX.at[2], mhs.at[1], mhr.at[1], s - 1, me).wait_send()
        copy(PA.at[0], PR.at[1], pss.at[1], prs.at[1], s - 1, me).wait_send()

    @pl.loop(0, nz)
    def _(c):
        halo(0, c, False)
        halo(1, c, False)

    for g in range(2):
        copy(RB.at[g, 1 - core], RP.at[g], r1s.at[g], r1r.at[g], partner, me).wait_send()
        chips(g, False)
        copy(GF.at[g, core], GF.at[g, core], r3s.at[g], r3r.at[g], partner, me).wait_send()


def store(gf_ref, g1_ref, g2_ref, gf_hbm, g1_hbm, g2_hbm, sems):
    rows = g1_hbm.shape[0]
    copies = [
        pltpu.make_async_copy(g1_ref.at[0:rows], g1_hbm, sems.at[0]),
        pltpu.make_async_copy(g2_ref.at[0:rows], g2_hbm, sems.at[1]),
        pltpu.make_async_copy(gf_ref, gf_hbm, sems.at[2]),
    ]
    for c in copies:
        c.start()
    for c in copies:
        c.wait()


def up(value, step):
    return -(-value // step) * step


def body(n, nz, feats, grads, mask, w_first, w_second):
    cb, _, ys, zs = feats.shape
    taps, full, _ = w_first.shape
    cells = ys * zs
    ex = (ys + 2) * zs
    mz = mask.shape[2]
    scale = float((n * ys * zs) ** -0.5)
    rows = taps * cb
    half = up(-(-rows // 2), 16)
    cp = up(cb, 16)
    kb = up(nz * cp, 128)
    kc = up(full, 128)
    vm = pltpu.VMEM
    dma = pltpu.SemaphoreType.DMA
    spec = pl.BlockSpec(memory_space=pltpu.VMEM)
    hbm = pl.BlockSpec(memory_space=pltpu.HBM)
    flat = (cb * ys, zs)
    split = (zs // 128, cb * ys, 128)
    gf, g1, g2 = pl.pallas_call(
        functools.partial(kernel, n, nz, cb, ys, zs, scale, "space", "chan"),
        out_shape=(
            jax.ShapeDtypeStruct(flat, BF16),
            jax.ShapeDtypeStruct((2 * half, full), F32),
            jax.ShapeDtypeStruct((2 * half, full), F32),
        ),
        in_specs=[hbm] * 5,
        out_specs=(spec,) * 3,
        scratch_shapes=[
            vm((taps, full, full), BF16), vm((taps, full, full), BF16), vm((ys, mz), jnp.int32), dma((5,)),
            vm((2, 3, nz, *flat), BF16),
            vm((nz, ys, zs), F32),
            vm((3, ys, zs), F32),
            vm((2, 3, kb, ex), BF16),
            vm((3 * full, 9 * kb), BF16),
            vm((3 * full, 9 * kb), BF16),
            vm((9 * cb, 3 * kc), F32),
            vm((9 * cb, 3 * kc), BF16),
            vm((nz, *split), F32),
            vm((full, cells), BF16),
            vm((full, cells), F32),
            vm((full, cells), F32),
            vm((kc, ex), BF16),
            vm((9 * cb, cells), F32),
            vm((3, 9 * cb, cells), BF16),
            vm((3, *split), F32),
            vm((2, *flat), BF16),
            vm((2, *flat), BF16),
            vm((2, 2 * half, full), F32),
            vm((2, 2, half, full), BF16),
            vm((2, half, full), BF16),
            vm((2, n // 2, half, full), BF16),
            vm((2, 2, half, full), F32),
            dma((2, nz)), dma((2, nz)), dma((2, 2, nz)), dma((2, 2, nz)),
            dma((nz,)), dma((nz,)), dma((2,)), dma((2,)), dma((2,)), dma((2,)),
            dma((2,)), dma((2,)), dma((2, n // 2)), dma((2, n // 2)), dma((2,)), dma((2,)),
        ],
        compiler_params=pltpu.CompilerParams(
            collective_id=0, has_side_effects=True, vmem_limit_bytes=48 << 20
        ),
    )(*(pltpu.with_memory_space_constraint(x, pltpu.HBM) for x in (
        feats.reshape(flat), grads.reshape(flat), mask.reshape(ys, mz), w_first, w_second)))
    gf, g1, g2 = pl.pallas_call(
        store,
        out_shape=(
            jax.ShapeDtypeStruct(flat, BF16),
            jax.ShapeDtypeStruct((rows, full), F32),
            jax.ShapeDtypeStruct((rows, full), F32),
        ),
        in_specs=[spec] * 3,
        out_specs=(hbm,) * 3,
        scratch_shapes=[dma((3,))],
    )(*(pltpu.with_memory_space_constraint(x, pltpu.VMEM) for x in (gf, g1, g2)))
    return (
        gf.reshape(cb, 1, ys, zs),
        g1.reshape(taps, cb, full).transpose(0, 2, 1),
        g2.reshape(taps, cb, full).transpose(0, 2, 1),
    )


def solution(mesh):
    in_specs = (
        P("chan", "space", None, None),
        P("chan", "space", None, None),
        P("space", None, "chan"),
        P(),
        P(),
    )
    out_specs = (P("chan", "space", None, None), P(None, None, "chan"), P(None, None, "chan"))
    sizes = (mesh.shape["space"], mesh.shape["chan"])
    return jax.shard_map(
        functools.partial(body, *sizes),
        mesh=mesh, in_specs=in_specs, out_specs=out_specs, check_vma=False,
    )
```

```python
import functools

import jax
import jax.numpy as jnp
from jax import lax
from jax.experimental import pallas as pl
from jax.experimental.pallas import tpu as pltpu
from jax.sharding import PartitionSpec as P

MESH = pl.DeviceIdType.MESH
F32 = jnp.float32
BF16 = jnp.bfloat16


def dot_nn(left, right):
    return jnp.dot(left, right, preferred_element_type=F32)


def dot_nt(left, right):
    return lax.dot_general(left, right, (((1,), (1,)), ((), ())), preferred_element_type=F32)


def one_hot(rows, cols, target):
    r = lax.broadcasted_iota(jnp.int32, (rows, cols), 0)
    q = lax.broadcasted_iota(jnp.int32, (rows, cols), 1)
    return jnp.where(target(r, q), 1.0, 0.0).astype(BF16)


def lane_shift(x, s):
    if s == 0:
        return x
    n = x.shape[1]
    z = lax.broadcasted_iota(jnp.int32, x.shape, 1)
    if s == 1:
        return jnp.where(z < n - 1, pltpu.roll(x, n - 1, 1), 0.0)
    return jnp.where(z > 0, pltpu.roll(x, 1, 1), 0.0)


def spread(out_ref, rows_of, cb, ys, zs):
    for y in range(ys):
        row = rows_of(y)
        for c in (-1, 0, 1):
            moved = lane_shift(row, -c)
            for b in (-1, 0, 1):
                j = 3 * (b + 1) + (c + 1)
                if 0 <= y + b < ys:
                    out_ref[j * cb : (j + 1) * cb, (y + b) * zs : (y + b + 1) * zs] = moved
    edge = jnp.zeros((3 * cb, zs), F32)
    out_ref[0 : 3 * cb, (ys - 1) * zs : ys * zs] = edge
    out_ref[6 * cb : 9 * cb, 0:zs] = edge


def kernel(
    n, nz, cb, ys, zs, scale, sp, ch_name,
    f_hbm, g_hbm, mask_hbm, w1_hbm, w2_hbm,
    gf_ref, g1_ref, g2_ref,
    w1_ref, w2_ref, mi_ref, ws, B, MK, MX, X, WA, WB, WCF, WC, TR, AC, SL, GPF, GP, SH, SM, TA, PA, PR,
    R32, PK, RB, RP, CS, GF,
    zss, zrs, hss, hrs, mss, mrs, mhs, mhr, pss, prs, r1s, r1r, r2s, r2r, r3s, r3r,
):
    s = lax.axis_index(sp)
    me = lax.axis_index(ch_name)
    full = w1_ref.shape[1]
    cells = ys * zs
    kb = X.shape[2]
    kc = GP.shape[0]
    cp = -(-cb // 16) * 16
    mz = mi_ref.shape[1]
    rows = 27 * cb
    main, rest = 21 * cb, 6 * cb
    half = RB.shape[2]
    ry = max(1, 256 // zs)
    nch = n // 2
    tiles = zs // 128
    core = lax.rem(s, 2)
    chip = lax.div(s, 2)
    partner = s + 1 - 2 * core
    left, right = s > 0, s < n - 1

    def copy(src, dst, ssem, rsem, ds, dc):
        return pltpu.make_async_remote_copy(
            src_ref=src, dst_ref=dst, send_sem=ssem, recv_sem=rsem,
            device_id=(ds, dc), device_id_type=MESH,
        )

    load_m = pltpu.make_async_copy(mask_hbm, mi_ref, ws.at[2])
    load_f = pltpu.make_async_copy(f_hbm, B.at[0, 1, me], ws.at[3])
    load_g = pltpu.make_async_copy(g_hbm, B.at[1, 1, me], ws.at[4])
    load1 = pltpu.make_async_copy(w1_hbm, w1_ref, ws.at[0])
    load2 = pltpu.make_async_copy(w2_hbm, w2_ref, ws.at[1])
    load_m.start()
    load_f.start()
    load_g.start()
    load1.start()
    load2.start()
    barrier = pltpu.get_barrier_semaphore()

    @pl.loop(1, nz)
    def _(i):
        pl.semaphore_signal(barrier, inc=1, device_id=(s, lax.rem(me + i, nz)), device_id_type=MESH)

    @pl.loop(1, n)
    def _(i):
        pl.semaphore_signal(barrier, inc=1, device_id=(lax.rem(s + i, n), me), device_id_type=MESH)

    for kind in range(2):
        X[kind] = jnp.zeros(X.shape[1:], BF16)
    GP[...] = jnp.zeros(GP.shape, BF16)
    WCF[...] = jnp.zeros(WCF.shape, F32)
    PK[...] = jnp.zeros(PK.shape, F32)
    load_m.wait()
    place = one_hot(mz, zs, lambda r, q: q == r + mz * me)
    MK[me] = dot_nn(mi_ref[...].astype(F32).astype(BF16), place)
    load_f.wait()
    load_g.wait()
    pl.semaphore_wait(barrier, n + nz - 2)

    def z_copy(i, buf, ssem, rsem):
        return copy(buf, buf, ssem.at[i], rsem.at[i], s, lax.rem(me + i, nz))

    order = sorted(range(1, nz), key=lambda i: min(i, nz - i))
    for i in order:
        z_copy(i, MK.at[me], mss, mrs).start()
    for kind in range(2):
        for i in order:
            z_copy(i, B.at[kind, 1, me], zss.at[kind], zrs.at[kind]).start()

    def halo(kind, c, start):
        src = B.at[kind, 1, c]

        @pl.when(right)
        def _():
            d = copy(src, B.at[kind, 0, c], hss.at[kind, 0, c], hrs.at[kind, 0, c], s + 1, me)
            d.start() if start else d.wait_send()

        @pl.when(left)
        def _():
            d = copy(src, B.at[kind, 2, c], hss.at[kind, 1, c], hrs.at[kind, 1, c], s - 1, me)
            d.start() if start else d.wait_send()

    halo(1, me, True)
    halo(0, me, True)

    load1.wait()
    load2.wait()
    pick = one_hot(cb, full, lambda r, q: q == r + cb * me)
    same = one_hot(full, full, lambda r, q: q == r)
    widen = one_hot(kb, full, lambda r, q: r == (q // cb) * cp + lax.rem(q, cb))
    for a in range(3):
        for b in range(3):
            lanes = slice((3 * a + b) * kb, (3 * a + b + 1) * kb)
            for c in range(3):
                k = 9 * a + 3 * b + c
                w1 = w1_ref[k]
                wide = dot_nn(widen, w1).astype(BF16)
                WA[c * full : (c + 1) * full, lanes] = dot_nt(same, wide).astype(BF16)
                WB[c * full : (c + 1) * full, lanes] = dot_nt(w2_ref[k], widen).astype(BF16)
                WCF[(3 * a + c) * cb : (3 * a + c + 1) * cb, b * kc : b * kc + full] = dot_nn(pick, w1)
    WC[...] = WCF[...].astype(BF16)

    for i in order:
        c = lax.rem(me + nz - i, nz)
        copy(MK.at[c], MK.at[c], mss.at[i], mrs.at[i], s, c).wait_recv()
    own_mask = MK[0]
    for c in range(1, nz):
        own_mask = own_mask + MK[c]
    MX[1] = own_mask

    @pl.when(right)
    def _():
        copy(MX.at[1], MX.at[0], mhs.at[0], mhr.at[0], s + 1, me).start()

    @pl.when(left)
    def _():
        copy(MX.at[1], MX.at[2], mhs.at[1], mhr.at[1], s - 1, me).start()

    def native(kind, slab, c):
        x = B[kind, slab, c].astype(F32)
        if kind:
            x = (x.reshape(cb, ys, zs) * MX[slab][None]).reshape(cb * ys, zs)
        return x

    def put(ref, x):
        for q in range(tiles):
            ref[q] = x[:, q * 128 : (q + 1) * 128]

    def take(ref, y):
        return jnp.concatenate([ref[q, pl.ds(y, cb, stride=ys), :] for q in range(tiles)], axis=1)

    def whole(ref):
        return jnp.concatenate([ref[q] for q in range(tiles)], axis=1)

    def relayout(kind, slab, c, t):
        put(TR.at[t], native(kind, slab, c))
        at = pl.ds(pl.multiple_of(c * cp, 16), cb)
        for y in range(ys):
            X[kind, slab, at, (1 + y) * zs : (2 + y) * zs] = take(TR.at[t], y).astype(BF16)

    def arrive(kind):
        for i in order:
            c = lax.rem(me + nz - i, nz)
            copy(B.at[kind, 1, c], B.at[kind, 1, c], zss.at[kind, i], zrs.at[kind, i], s, c).wait_recv()
            halo(kind, c, True)
            relayout(kind, 1, c, i)

    def arrive_halo(kind):
        for side, slab, there in ((0, 0, left), (1, 2, right)):

            @pl.when(there)
            def _():
                for c in range(nz):
                    copy(B.at[kind, slab, c], B.at[kind, slab, c], hss.at[kind, side, c], hrs.at[kind, side, c], s, me).wait_recv()
                    relayout(kind, slab, c, c)

    def conv(kind, W, step, direction):
        for y0 in range(0, ys, ry):
            parts = []
            for a in range(3):
                slab = a if direction == 1 else 2 - a
                for b in range(3):
                    y = y0 + 1 + direction * (b - 1)
                    parts.append(X[kind, slab, :, y * zs : (y + ry) * zs])
            res = dot_nn(W[...], jnp.concatenate(parts, axis=0))
            for r in range(ry):
                acc = None
                for c in range(3):
                    piece = lane_shift(res[c * full : (c + 1) * full, r * zs : (r + 1) * zs], direction * (c - 1))
                    acc = piece if acc is None else acc + piece
                step(y0 + r, acc)

    relayout(0, 1, me, 0)
    arrive(0)
    relayout(1, 1, me, 0)
    arrive(1)

    def spread_masked(slab):
        put(TR.at[0], native(1, slab, me))
        spread(SH, lambda y: take(TR.at[0], y), cb, ys, zs)
        SM[2 - slab] = SH[...].astype(BF16)

    spread_masked(1)
    for side, slab, there in ((0, 0, left), (1, 2, right)):

        @pl.when(there)
        def _():
            copy(MX.at[slab], MX.at[slab], mhs.at[side], mhr.at[side], s, me).wait_recv()
            copy(B.at[1, slab, me], B.at[1, slab, me], hss.at[1, side, me], hrs.at[1, side, me], s, me).wait_recv()
            spread_masked(slab)
            relayout(1, slab, me, 0)

        @pl.when(jnp.logical_not(there))
        def _():
            SM[2 - slab] = jnp.zeros(SM.shape[1:], BF16)

    arrive_halo(0)

    def pre_step(y, acc):
        at = slice(y * zs, (y + 1) * zs)
        m = MX[1, y : y + 1, :]
        pre = acc * m
        sig = jax.nn.sigmoid(pre)
        AC[:, at] = (pre * sig).astype(BF16)
        SL[:, at] = sig * (1.0 + pre * (1.0 - sig)) * m

    conv(0, WA, pre_step, 1)

    def pair_start(g):
        PK[g, 0:main, 0:full] = R32[g, 0:main, :]
        for p in range(3):
            PK[g, p * rest : (p + 1) * rest, full:128] = R32[g, main:rows, 32 * p : 32 * p + 32]
        RB[g] = PK[g].astype(BF16).reshape(RB.shape[1:])
        copy(RB.at[g, 1 - core], RP.at[g], r1s.at[g], r1r.at[g], partner, me).start()

    def chips(g, start):
        @pl.loop(1, nch)
        def _(i):
            to = lax.rem(chip + i, nch)
            d = copy(CS.at[g, chip], CS.at[g, chip], r2s.at[g, i], r2r.at[g, i], 2 * to + core, me)
            d.start() if start else d.wait_send()

    def chip_sum(g):
        copy(RP.at[g], RP.at[g], r1s.at[g], r1r.at[g], partner, me).wait_recv()
        mine = PK[g, pl.ds(pl.multiple_of(core * half, 8), half), :]
        CS[g, chip] = (mine + RP[g].astype(F32)).astype(BF16)
        chips(g, True)

    def total(g):
        @pl.loop(1, nch)
        def _(i):
            j = lax.rem(chip + nch - i, nch)
            copy(CS.at[g, j], CS.at[g, j], r2s.at[g, i], r2r.at[g, i], s, me).wait_recv()

        acc = CS[g, 0].astype(F32)
        for j in range(1, nch):
            acc = acc + CS[g, j].astype(F32)
        GF[g, core] = acc
        copy(GF.at[g, core], GF.at[g, core], r3s.at[g], r3r.at[g], partner, me).start()

    def finish(g, out_ref):
        other = GF.at[g, 1 - core]
        copy(other, other, r3s.at[g], r3r.at[g], partner, me).wait_recv()
        done = GF[g].reshape(PK.shape[1:])
        out_ref[0:main, :] = done[0:main, 0:full]
        for p in range(3):
            out_ref[main:rows, 32 * p : 32 * p + 32] = done[p * rest : (p + 1) * rest, full:128]

    for a in range(3):
        R32[1, 9 * cb * a : 9 * cb * (a + 1), :] = dot_nt(SM[a], AC[...]) * scale
    pair_start(1)

    def wait_halo_grads():
        for side, slab, there in ((0, 0, left), (1, 2, right)):

            @pl.when(there)
            def _():
                @pl.loop(1, nz)
                def _(i):
                    c = lax.rem(me + i, nz)
                    copy(B.at[1, slab, c], B.at[1, slab, c], hss.at[1, side, c], hrs.at[1, side, c], s, me).wait_recv()
                    relayout(1, slab, c, i)

    chip_sum(1)
    wait_halo_grads()

    def back_step(y, acc):
        gp = acc * SL[:, y * zs : (y + 1) * zs]
        GPF[:, y * zs : (y + 1) * zs] = gp
        GP[0:full, (1 + y) * zs : (2 + y) * zs] = gp.astype(BF16)

    conv(1, WB, back_step, -1)

    own_rows = pl.ds(pl.multiple_of(me * cb, 8), cb)
    spread(SH, lambda y: GPF[own_rows, y * zs : (y + 1) * zs], cb, ys, zs)
    moved = SH[...].astype(BF16)
    narrow = one_hot(full, kb, lambda r, q: q == (r // cb) * cp + lax.rem(r, cb))
    for a in range(3):
        wide = (dot_nt(moved, X[0, a, :, zs : zs + cells]) * scale).astype(BF16)
        R32[0, 9 * cb * a : 9 * cb * (a + 1), :] = dot_nt(wide, narrow)
    pair_start(0)

    for y0 in range(0, ys, ry):
        parts = []
        for b in range(3):
            y = y0 + 1 - (b - 1)
            parts.append(GP[:, y * zs : (y + ry) * zs])
        res = dot_nn(WC[...], jnp.concatenate(parts, axis=0))
        for a in range(3):
            for r in range(ry):
                acc = None
                for c in range(3):
                    j = 3 * a + c
                    piece = lane_shift(res[j * cb : (j + 1) * cb, r * zs : (r + 1) * zs], -(c - 1))
                    acc = piece if acc is None else acc + piece
                for q in range(tiles):
                    TA[a, q, pl.ds(y0 + r, cb, stride=ys), :] = acc[:, q * 128 : (q + 1) * 128]
    PA[0] = whole(TA.at[0]).astype(BF16)
    PA[1] = whole(TA.at[2]).astype(BF16)

    @pl.when(right)
    def _():
        copy(PA.at[1], PR.at[0], pss.at[0], prs.at[0], s + 1, me).start()

    @pl.when(left)
    def _():
        copy(PA.at[0], PR.at[1], pss.at[1], prs.at[1], s - 1, me).start()

    chip_sum(0)
    total(1)

    for side, there in ((0, left), (1, right)):

        @pl.when(there)
        def _():
            copy(PR.at[side], PR.at[side], pss.at[side], prs.at[side], s, me).wait_recv()
            put(TA.at[1], whole(TA.at[1]) + PR[side].astype(F32))

    gf = whole(TA.at[1]).reshape(cb, ys, zs) * MX[1][None]
    gf_ref[...] = gf.reshape(cb * ys, zs).astype(BF16)

    finish(1, g2_ref)
    total(0)
    finish(0, g1_ref)

    for i in order:
        z_copy(i, MK.at[me], mss, mrs).wait_send()
        for kind in range(2):
            z_copy(i, B.at[kind, 1, me], zss.at[kind], zrs.at[kind]).wait_send()

    @pl.when(right)
    def _():
        copy(MX.at[1], MX.at[0], mhs.at[0], mhr.at[0], s + 1, me).wait_send()
        copy(PA.at[1], PR.at[0], pss.at[0], prs.at[0], s + 1, me).wait_send()

    @pl.when(left)
    def _():
        copy(MX.at[1], MX.at[2], mhs.at[1], mhr.at[1], s - 1, me).wait_send()
        copy(PA.at[0], PR.at[1], pss.at[1], prs.at[1], s - 1, me).wait_send()

    @pl.loop(0, nz)
    def _(c):
        halo(0, c, False)
        halo(1, c, False)

    for g in range(2):
        copy(RB.at[g, 1 - core], RP.at[g], r1s.at[g], r1r.at[g], partner, me).wait_send()
        chips(g, False)
        copy(GF.at[g, core], GF.at[g, core], r3s.at[g], r3r.at[g], partner, me).wait_send()


def store(gf_ref, g1_ref, g2_ref, gf_hbm, g1_hbm, g2_hbm, sems):
    copies = [
        pltpu.make_async_copy(g1_ref, g1_hbm, sems.at[0]),
        pltpu.make_async_copy(g2_ref, g2_hbm, sems.at[1]),
        pltpu.make_async_copy(gf_ref, gf_hbm, sems.at[2]),
    ]
    for c in copies:
        c.start()
    for c in copies:
        c.wait()


def up(value, step):
    return -(-value // step) * step


def body(n, nz, feats, grads, mask, w_first, w_second):
    cb, _, ys, zs = feats.shape
    taps, full, _ = w_first.shape
    cells = ys * zs
    ex = (ys + 2) * zs
    mz = mask.shape[2]
    scale = float((n * ys * zs) ** -0.5)
    rows = taps * cb
    half = up(-(-21 * cb // 2), 16)
    cp = up(cb, 16)
    kb = up(nz * cp, 128)
    kc = up(full, 128)
    vm = pltpu.VMEM
    dma = pltpu.SemaphoreType.DMA
    spec = pl.BlockSpec(memory_space=pltpu.VMEM)
    hbm = pl.BlockSpec(memory_space=pltpu.HBM)
    flat = (cb * ys, zs)
    split = (zs // 128, cb * ys, 128)
    gf, g1, g2 = pl.pallas_call(
        functools.partial(kernel, n, nz, cb, ys, zs, scale, "space", "chan"),
        out_shape=(
            jax.ShapeDtypeStruct(flat, BF16),
            jax.ShapeDtypeStruct((rows, full), F32),
            jax.ShapeDtypeStruct((rows, full), F32),
        ),
        in_specs=[hbm] * 5,
        out_specs=(spec,) * 3,
        scratch_shapes=[
            vm((taps, full, full), BF16), vm((taps, full, full), BF16), vm((ys, mz), jnp.int32), dma((5,)),
            vm((2, 3, nz, *flat), BF16),
            vm((nz, ys, zs), F32),
            vm((3, ys, zs), F32),
            vm((2, 3, kb, ex), BF16),
            vm((3 * full, 9 * kb), BF16),
            vm((3 * full, 9 * kb), BF16),
            vm((9 * cb, 3 * kc), F32),
            vm((9 * cb, 3 * kc), BF16),
            vm((nz + 1, *split), F32),
            vm((full, cells), BF16),
            vm((full, cells), F32),
            vm((full, cells), F32),
            vm((kc, ex), BF16),
            vm((9 * cb, cells), F32),
            vm((3, 9 * cb, cells), BF16),
            vm((3, *split), F32),
            vm((2, *flat), BF16),
            vm((2, *flat), BF16),
            vm((2, rows, full), F32),
            vm((2, 2 * half, 128), F32),
            vm((2, 2, half, 128), BF16),
            vm((2, half, 128), BF16),
            vm((2, n // 2, half, 128), BF16),
            vm((2, 2, half, 128), F32),
            dma((2, nz)), dma((2, nz)), dma((2, 2, nz)), dma((2, 2, nz)),
            dma((nz,)), dma((nz,)), dma((2,)), dma((2,)), dma((2,)), dma((2,)),
            dma((2,)), dma((2,)), dma((2, n // 2)), dma((2, n // 2)), dma((2,)), dma((2,)),
        ],
        compiler_params=pltpu.CompilerParams(
            collective_id=0, has_side_effects=True, vmem_limit_bytes=48 << 20
        ),
    )(*(pltpu.with_memory_space_constraint(x, pltpu.HBM) for x in (
        feats.reshape(flat), grads.reshape(flat), mask.reshape(ys, mz), w_first, w_second)))
    gf, g1, g2 = pl.pallas_call(
        store,
        out_shape=(
            jax.ShapeDtypeStruct(flat, BF16),
            jax.ShapeDtypeStruct((rows, full), F32),
            jax.ShapeDtypeStruct((rows, full), F32),
        ),
        in_specs=[spec] * 3,
        out_specs=(hbm,) * 3,
        scratch_shapes=[dma((3,))],
    )(*(pltpu.with_memory_space_constraint(x, pltpu.VMEM) for x in (gf, g1, g2)))
    return (
        gf.reshape(cb, 1, ys, zs),
        g1.reshape(taps, cb, full).transpose(0, 2, 1),
        g2.reshape(taps, cb, full).transpose(0, 2, 1),
    )


def solution(mesh):
    in_specs = (
        P("chan", "space", None, None),
        P("chan", "space", None, None),
        P("space", None, "chan"),
        P(),
        P(),
    )
    out_specs = (P("chan", "space", None, None), P(None, None, "chan"), P(None, None, "chan"))
    sizes = (mesh.shape["space"], mesh.shape["chan"])
    return jax.shard_map(
        functools.partial(body, *sizes),
        mesh=mesh, in_specs=in_specs, out_specs=out_specs, check_vma=False,
    )
```

```python
import functools

import jax
import jax.numpy as jnp
from jax import lax
from jax.experimental import pallas as pl
from jax.experimental.pallas import tpu as pltpu
from jax.sharding import PartitionSpec as P

MESH = pl.DeviceIdType.MESH
F32 = jnp.float32
BF16 = jnp.bfloat16


def dot_nn(left, right):
    return jnp.dot(left, right, preferred_element_type=F32)


def dot_nt(left, right):
    return lax.dot_general(left, right, (((1,), (1,)), ((), ())), preferred_element_type=F32)


def one_hot(rows, cols, target):
    r = lax.broadcasted_iota(jnp.int32, (rows, cols), 0)
    q = lax.broadcasted_iota(jnp.int32, (rows, cols), 1)
    return jnp.where(target(r, q), 1.0, 0.0).astype(BF16)


def lane_shift(x, s):
    if s == 0:
        return x
    n = x.shape[1]
    z = lax.broadcasted_iota(jnp.int32, x.shape, 1)
    if s == 1:
        return jnp.where(z < n - 1, pltpu.roll(x, n - 1, 1), 0.0)
    return jnp.where(z > 0, pltpu.roll(x, 1, 1), 0.0)


def spread(out_ref, rows_of, cb, ys, zs):
    for y in range(ys):
        row = rows_of(y)
        for c in (-1, 0, 1):
            moved = lane_shift(row, -c)
            for b in (-1, 0, 1):
                j = 3 * (b + 1) + (c + 1)
                if 0 <= y + b < ys:
                    out_ref[j * cb : (j + 1) * cb, (y + b) * zs : (y + b + 1) * zs] = moved
    edge = jnp.zeros((3 * cb, zs), F32)
    out_ref[0 : 3 * cb, (ys - 1) * zs : ys * zs] = edge
    out_ref[6 * cb : 9 * cb, 0:zs] = edge


def kernel(
    n, nz, cb, ys, zs, scale, sp, ch_name,
    f_hbm, g_hbm, mask_hbm, w1_hbm, w2_hbm,
    gf_ref, g1_ref, g2_ref,
    w1_ref, w2_ref, mi_ref, ws, B, MK, MX, X, WA, WB, WCF, WC, TR, AC, SL, GPF, GP, SH, SM, TA, PA, PR,
    R32, PK, RB, RP, CS, GF,
    zss, zrs, hss, hrs, mss, mrs, mhs, mhr, pss, prs, r1s, r1r, r2s, r2r, r3s, r3r,
):
    s = lax.axis_index(sp)
    me = lax.axis_index(ch_name)
    full = w1_ref.shape[1]
    cells = ys * zs
    kb = X.shape[2]
    kc = GP.shape[0]
    cp = -(-cb // 16) * 16
    mz = mi_ref.shape[1]
    rows = 27 * cb
    main, rest = 21 * cb, 6 * cb
    half = RB.shape[2]
    ry = max(1, 256 // zs)
    nch = n // 2
    tiles = zs // 128
    core = lax.rem(s, 2)
    chip = lax.div(s, 2)
    partner = s + 1 - 2 * core
    left, right = s > 0, s < n - 1

    def copy(src, dst, ssem, rsem, ds, dc):
        return pltpu.make_async_remote_copy(
            src_ref=src, dst_ref=dst, send_sem=ssem, recv_sem=rsem,
            device_id=(ds, dc), device_id_type=MESH,
        )

    load_m = pltpu.make_async_copy(mask_hbm, mi_ref, ws.at[2])
    load_f = pltpu.make_async_copy(f_hbm, B.at[0, 1, me], ws.at[3])
    load_g = pltpu.make_async_copy(g_hbm, B.at[1, 1, me], ws.at[4])
    load1 = pltpu.make_async_copy(w1_hbm, w1_ref, ws.at[0])
    load2 = pltpu.make_async_copy(w2_hbm, w2_ref, ws.at[1])
    load_m.start()
    load_f.start()
    load_g.start()
    load1.start()
    load2.start()
    barrier = pltpu.get_barrier_semaphore()

    @pl.loop(1, nz)
    def _(i):
        pl.semaphore_signal(barrier, inc=1, device_id=(s, lax.rem(me + i, nz)), device_id_type=MESH)

    @pl.loop(1, n)
    def _(i):
        pl.semaphore_signal(barrier, inc=1, device_id=(lax.rem(s + i, n), me), device_id_type=MESH)

    load_m.wait()
    place = one_hot(mz, zs, lambda r, q: q == r + mz * me)
    MK[me] = dot_nn(mi_ref[...].astype(F32).astype(BF16), place)
    load_f.wait()
    load_g.wait()
    pl.semaphore_wait(barrier, n + nz - 2)

    def z_copy(i, buf, ssem, rsem):
        return copy(buf, buf, ssem.at[i], rsem.at[i], s, lax.rem(me + i, nz))

    order = sorted(range(1, nz), key=lambda i: min(i, nz - i))
    for i in order:
        z_copy(i, MK.at[me], mss, mrs).start()
    for kind in range(2):
        for to in range(nz):

            @pl.when(me != to)
            def _():
                z_copy(lax.rem(to - me + nz, nz), B.at[kind, 1, me], zss.at[kind], zrs.at[kind]).start()

    def halo(kind, c, start):
        src = B.at[kind, 1, c]

        @pl.when(right)
        def _():
            d = copy(src, B.at[kind, 0, c], hss.at[kind, 0, c], hrs.at[kind, 0, c], s + 1, me)
            d.start() if start else d.wait_send()

        @pl.when(left)
        def _():
            d = copy(src, B.at[kind, 2, c], hss.at[kind, 1, c], hrs.at[kind, 1, c], s - 1, me)
            d.start() if start else d.wait_send()

    halo(1, me, True)
    halo(0, me, True)

    for kind in range(2):
        X[kind] = jnp.zeros(X.shape[1:], BF16)
    GP[...] = jnp.zeros(GP.shape, BF16)
    WCF[...] = jnp.zeros(WCF.shape, F32)
    PK[...] = jnp.zeros(PK.shape, F32)
    load1.wait()
    load2.wait()
    pick = one_hot(cb, full, lambda r, q: q == r + cb * me)
    same = one_hot(full, full, lambda r, q: q == r)
    widen = one_hot(kb, full, lambda r, q: r == (q // cb) * cp + lax.rem(q, cb))
    for a in range(3):
        for b in range(3):
            lanes = slice((3 * a + b) * kb, (3 * a + b + 1) * kb)
            for c in range(3):
                k = 9 * a + 3 * b + c
                w1 = w1_ref[k]
                wide = dot_nn(widen, w1).astype(BF16)
                WA[c * full : (c + 1) * full, lanes] = dot_nt(same, wide).astype(BF16)
                WB[c * full : (c + 1) * full, lanes] = dot_nt(w2_ref[k], widen).astype(BF16)
                WCF[(3 * a + c) * cb : (3 * a + c + 1) * cb, b * kc : b * kc + full] = dot_nn(pick, w1)
    WC[...] = WCF[...].astype(BF16)

    for i in order:
        c = lax.rem(me + nz - i, nz)
        copy(MK.at[c], MK.at[c], mss.at[i], mrs.at[i], s, c).wait_recv()
    own_mask = MK[0]
    for c in range(1, nz):
        own_mask = own_mask + MK[c]
    MX[1] = own_mask

    @pl.when(right)
    def _():
        copy(MX.at[1], MX.at[0], mhs.at[0], mhr.at[0], s + 1, me).start()

    @pl.when(left)
    def _():
        copy(MX.at[1], MX.at[2], mhs.at[1], mhr.at[1], s - 1, me).start()

    def native(kind, slab, c):
        x = B[kind, slab, c].astype(F32)
        if kind:
            x = (x.reshape(cb, ys, zs) * MX[slab][None]).reshape(cb * ys, zs)
        return x

    def put(ref, x):
        for q in range(tiles):
            ref[q] = x[:, q * 128 : (q + 1) * 128]

    def take(ref, y):
        return jnp.concatenate([ref[q, pl.ds(y, cb, stride=ys), :] for q in range(tiles)], axis=1)

    def whole(ref):
        return jnp.concatenate([ref[q] for q in range(tiles)], axis=1)

    def relayout(kind, slab, c, t):
        put(TR.at[t], native(kind, slab, c))
        at = pl.ds(pl.multiple_of(c * cp, 16), cb)
        for y in range(ys):
            X[kind, slab, at, (1 + y) * zs : (2 + y) * zs] = take(TR.at[t], y).astype(BF16)

    def arrive(kind):
        for i in order:
            c = lax.rem(me + nz - i, nz)
            copy(B.at[kind, 1, c], B.at[kind, 1, c], zss.at[kind, i], zrs.at[kind, i], s, c).wait_recv()
            halo(kind, c, True)
            relayout(kind, 1, c, i)

    def arrive_halo(kind):
        for side, slab, there in ((0, 0, left), (1, 2, right)):

            @pl.when(there)
            def _():
                for c in range(nz):
                    copy(B.at[kind, slab, c], B.at[kind, slab, c], hss.at[kind, side, c], hrs.at[kind, side, c], s, me).wait_recv()
                    relayout(kind, slab, c, c)

    def conv(kind, W, step, direction):
        for y0 in range(0, ys, ry):
            parts = []
            for a in range(3):
                slab = a if direction == 1 else 2 - a
                for b in range(3):
                    y = y0 + 1 + direction * (b - 1)
                    parts.append(X[kind, slab, :, y * zs : (y + ry) * zs])
            res = dot_nn(W[...], jnp.concatenate(parts, axis=0))
            for r in range(ry):
                acc = None
                for c in range(3):
                    piece = lane_shift(res[c * full : (c + 1) * full, r * zs : (r + 1) * zs], direction * (c - 1))
                    acc = piece if acc is None else acc + piece
                step(y0 + r, acc)

    relayout(0, 1, me, 0)
    arrive(0)
    def spread_masked(slab):
        put(TR.at[0], native(1, slab, me))
        spread(SH, lambda y: take(TR.at[0], y), cb, ys, zs)
        SM[2 - slab] = SH[...].astype(BF16)

    spread_masked(1)
    for side, slab, there in ((0, 0, left), (1, 2, right)):

        @pl.when(there)
        def _():
            copy(MX.at[slab], MX.at[slab], mhs.at[side], mhr.at[side], s, me).wait_recv()
            copy(B.at[1, slab, me], B.at[1, slab, me], hss.at[1, side, me], hrs.at[1, side, me], s, me).wait_recv()
            spread_masked(slab)

        @pl.when(jnp.logical_not(there))
        def _():
            SM[2 - slab] = jnp.zeros(SM.shape[1:], BF16)

    relayout(1, 1, me, 0)
    arrive(1)

    arrive_halo(0)

    def pre_step(y, acc):
        at = slice(y * zs, (y + 1) * zs)
        m = MX[1, y : y + 1, :]
        pre = acc * m
        sig = jax.nn.sigmoid(pre)
        AC[:, at] = (pre * sig).astype(BF16)
        SL[:, at] = sig * (1.0 + pre * (1.0 - sig)) * m

    conv(0, WA, pre_step, 1)

    def pair_start(g):
        PK[g, 0:main, 0:full] = R32[g, 0:main, :]
        for p in range(3):
            PK[g, p * rest : (p + 1) * rest, full:128] = R32[g, main:rows, 32 * p : 32 * p + 32]
        RB[g] = PK[g].astype(BF16).reshape(RB.shape[1:])
        copy(RB.at[g, 1 - core], RP.at[g], r1s.at[g], r1r.at[g], partner, me).start()

    def chips(g, start):
        @pl.loop(1, nch)
        def _(i):
            to = lax.rem(chip + i, nch)
            d = copy(CS.at[g, chip], CS.at[g, chip], r2s.at[g, i], r2r.at[g, i], 2 * to + core, me)
            d.start() if start else d.wait_send()

    def chip_sum(g):
        copy(RP.at[g], RP.at[g], r1s.at[g], r1r.at[g], partner, me).wait_recv()
        mine = PK[g, pl.ds(pl.multiple_of(core * half, 8), half), :]
        CS[g, chip] = (mine + RP[g].astype(F32)).astype(BF16)
        chips(g, True)

    def total(g):
        @pl.loop(1, nch)
        def _(i):
            j = lax.rem(chip + nch - i, nch)
            copy(CS.at[g, j], CS.at[g, j], r2s.at[g, i], r2r.at[g, i], s, me).wait_recv()

        acc = CS[g, 0].astype(F32)
        for j in range(1, nch):
            acc = acc + CS[g, j].astype(F32)
        GF[g, core] = acc
        copy(GF.at[g, core], GF.at[g, core], r3s.at[g], r3r.at[g], partner, me).start()

    def finish(g, out_ref):
        other = GF.at[g, 1 - core]
        copy(other, other, r3s.at[g], r3r.at[g], partner, me).wait_recv()
        done = GF[g].reshape(PK.shape[1:])
        out_ref[0:main, :] = done[0:main, 0:full]
        for p in range(3):
            out_ref[main:rows, 32 * p : 32 * p + 32] = done[p * rest : (p + 1) * rest, full:128]

    for a in range(3):
        R32[1, 9 * cb * a : 9 * cb * (a + 1), :] = dot_nt(SM[a], AC[...]) * scale
    pair_start(1)

    def wait_halo_grads():
        for side, slab, there in ((0, 0, left), (1, 2, right)):

            @pl.when(there)
            def _():
                relayout(1, slab, me, 0)

                @pl.loop(1, nz)
                def _(i):
                    c = lax.rem(me + i, nz)
                    copy(B.at[1, slab, c], B.at[1, slab, c], hss.at[1, side, c], hrs.at[1, side, c], s, me).wait_recv()
                    relayout(1, slab, c, i)

    chip_sum(1)
    wait_halo_grads()

    def back_step(y, acc):
        gp = acc * SL[:, y * zs : (y + 1) * zs]
        GPF[:, y * zs : (y + 1) * zs] = gp
        GP[0:full, (1 + y) * zs : (2 + y) * zs] = gp.astype(BF16)

    conv(1, WB, back_step, -1)

    own_rows = pl.ds(pl.multiple_of(me * cb, 8), cb)
    spread(SH, lambda y: GPF[own_rows, y * zs : (y + 1) * zs], cb, ys, zs)
    moved = SH[...].astype(BF16)
    narrow = one_hot(full, kb, lambda r, q: q == (r // cb) * cp + lax.rem(r, cb))
    for a in range(3):
        wide = (dot_nt(moved, X[0, a, :, zs : zs + cells]) * scale).astype(BF16)
        R32[0, 9 * cb * a : 9 * cb * (a + 1), :] = dot_nt(wide, narrow)
    pair_start(0)

    for y0 in range(0, ys, ry):
        parts = []
        for b in range(3):
            y = y0 + 1 - (b - 1)
            parts.append(GP[:, y * zs : (y + ry) * zs])
        res = dot_nn(WC[...], jnp.concatenate(parts, axis=0))
        for a in range(3):
            for r in range(ry):
                acc = None
                for c in range(3):
                    j = 3 * a + c
                    piece = lane_shift(res[j * cb : (j + 1) * cb, r * zs : (r + 1) * zs], -(c - 1))
                    acc = piece if acc is None else acc + piece
                for q in range(tiles):
                    TA[a, q, pl.ds(y0 + r, cb, stride=ys), :] = acc[:, q * 128 : (q + 1) * 128]
    PA[0] = whole(TA.at[0]).astype(BF16)
    PA[1] = whole(TA.at[2]).astype(BF16)

    chip_sum(0)

    @pl.when(right)
    def _():
        copy(PA.at[1], PR.at[0], pss.at[0], prs.at[0], s + 1, me).start()

    @pl.when(left)
    def _():
        copy(PA.at[0], PR.at[1], pss.at[1], prs.at[1], s - 1, me).start()

    total(1)

    total(0)
    for side, there in ((0, left), (1, right)):

        @pl.when(there)
        def _():
            copy(PR.at[side], PR.at[side], pss.at[side], prs.at[side], s, me).wait_recv()
            put(TA.at[1], whole(TA.at[1]) + PR[side].astype(F32))

    gf = whole(TA.at[1]).reshape(cb, ys, zs) * MX[1][None]
    gf_ref[...] = gf.reshape(cb * ys, zs).astype(BF16)

    finish(1, g2_ref)
    finish(0, g1_ref)

    for i in order:
        z_copy(i, MK.at[me], mss, mrs).wait_send()
        for kind in range(2):
            z_copy(i, B.at[kind, 1, me], zss.at[kind], zrs.at[kind]).wait_send()

    @pl.when(right)
    def _():
        copy(MX.at[1], MX.at[0], mhs.at[0], mhr.at[0], s + 1, me).wait_send()
        copy(PA.at[1], PR.at[0], pss.at[0], prs.at[0], s + 1, me).wait_send()

    @pl.when(left)
    def _():
        copy(MX.at[1], MX.at[2], mhs.at[1], mhr.at[1], s - 1, me).wait_send()
        copy(PA.at[0], PR.at[1], pss.at[1], prs.at[1], s - 1, me).wait_send()

    @pl.loop(0, nz)
    def _(c):
        halo(0, c, False)
        halo(1, c, False)

    for g in range(2):
        copy(RB.at[g, 1 - core], RP.at[g], r1s.at[g], r1r.at[g], partner, me).wait_send()
        chips(g, False)
        copy(GF.at[g, core], GF.at[g, core], r3s.at[g], r3r.at[g], partner, me).wait_send()


def store(gf_ref, g1_ref, g2_ref, gf_hbm, g1_hbm, g2_hbm, sems):
    copies = [
        pltpu.make_async_copy(g1_ref, g1_hbm, sems.at[0]),
        pltpu.make_async_copy(g2_ref, g2_hbm, sems.at[1]),
        pltpu.make_async_copy(gf_ref, gf_hbm, sems.at[2]),
    ]
    for c in copies:
        c.start()
    for c in copies:
        c.wait()


def up(value, step):
    return -(-value // step) * step


def body(n, nz, feats, grads, mask, w_first, w_second):
    cb, _, ys, zs = feats.shape
    taps, full, _ = w_first.shape
    cells = ys * zs
    ex = (ys + 2) * zs
    mz = mask.shape[2]
    scale = float((n * ys * zs) ** -0.5)
    rows = taps * cb
    half = up(-(-21 * cb // 2), 16)
    cp = up(cb, 16)
    kb = up(nz * cp, 128)
    kc = up(full, 128)
    vm = pltpu.VMEM
    dma = pltpu.SemaphoreType.DMA
    spec = pl.BlockSpec(memory_space=pltpu.VMEM)
    hbm = pl.BlockSpec(memory_space=pltpu.HBM)
    flat = (cb * ys, zs)
    split = (zs // 128, cb * ys, 128)
    gf, g1, g2 = pl.pallas_call(
        functools.partial(kernel, n, nz, cb, ys, zs, scale, "space", "chan"),
        out_shape=(
            jax.ShapeDtypeStruct(flat, BF16),
            jax.ShapeDtypeStruct((rows, full), F32),
            jax.ShapeDtypeStruct((rows, full), F32),
        ),
        in_specs=[hbm] * 5,
        out_specs=(spec,) * 3,
        scratch_shapes=[
            vm((taps, full, full), BF16), vm((taps, full, full), BF16), vm((ys, mz), jnp.int32), dma((5,)),
            vm((2, 3, nz, *flat), BF16),
            vm((nz, ys, zs), F32),
            vm((3, ys, zs), F32),
            vm((2, 3, kb, ex), BF16),
            vm((3 * full, 9 * kb), BF16),
            vm((3 * full, 9 * kb), BF16),
            vm((9 * cb, 3 * kc), F32),
            vm((9 * cb, 3 * kc), BF16),
            vm((nz + 1, *split), F32),
            vm((full, cells), BF16),
            vm((full, cells), F32),
            vm((full, cells), F32),
            vm((kc, ex), BF16),
            vm((9 * cb, cells), F32),
            vm((3, 9 * cb, cells), BF16),
            vm((3, *split), F32),
            vm((2, *flat), BF16),
            vm((2, *flat), BF16),
            vm((2, rows, full), F32),
            vm((2, 2 * half, 128), F32),
            vm((2, 2, half, 128), BF16),
            vm((2, half, 128), BF16),
            vm((2, n // 2, half, 128), BF16),
            vm((2, 2, half, 128), F32),
            dma((2, nz)), dma((2, nz)), dma((2, 2, nz)), dma((2, 2, nz)),
            dma((nz,)), dma((nz,)), dma((2,)), dma((2,)), dma((2,)), dma((2,)),
            dma((2,)), dma((2,)), dma((2, n // 2)), dma((2, n // 2)), dma((2,)), dma((2,)),
        ],
        compiler_params=pltpu.CompilerParams(
            collective_id=0, has_side_effects=True, vmem_limit_bytes=48 << 20
        ),
    )(*(pltpu.with_memory_space_constraint(x, pltpu.HBM) for x in (
        feats.reshape(flat), grads.reshape(flat), mask.reshape(ys, mz), w_first, w_second)))
    gf, g1, g2 = pl.pallas_call(
        store,
        out_shape=(
            jax.ShapeDtypeStruct(flat, BF16),
            jax.ShapeDtypeStruct((rows, full), F32),
            jax.ShapeDtypeStruct((rows, full), F32),
        ),
        in_specs=[spec] * 3,
        out_specs=(hbm,) * 3,
        scratch_shapes=[dma((3,))],
    )(*(pltpu.with_memory_space_constraint(x, pltpu.VMEM) for x in (gf, g1, g2)))
    return (
        gf.reshape(cb, 1, ys, zs),
        g1.reshape(taps, cb, full).transpose(0, 2, 1),
        g2.reshape(taps, cb, full).transpose(0, 2, 1),
    )


def solution(mesh):
    in_specs = (
        P("chan", "space", None, None),
        P("chan", "space", None, None),
        P("space", None, "chan"),
        P(),
        P(),
    )
    out_specs = (P("chan", "space", None, None), P(None, None, "chan"), P(None, None, "chan"))
    sizes = (mesh.shape["space"], mesh.shape["chan"])
    return jax.shard_map(
        functools.partial(body, *sizes),
        mesh=mesh, in_specs=in_specs, out_specs=out_specs, check_vma=False,
    )
```

```python
import functools

import jax
import jax.numpy as jnp
from jax import lax
from jax.experimental import pallas as pl
from jax.experimental.pallas import tpu as pltpu
from jax.sharding import PartitionSpec as P

MESH = pl.DeviceIdType.MESH
F32 = jnp.float32
BF16 = jnp.bfloat16


def dot_nn(left, right):
    return jnp.dot(left, right, preferred_element_type=F32)


def dot_nt(left, right):
    return lax.dot_general(left, right, (((1,), (1,)), ((), ())), preferred_element_type=F32)


def one_hot(rows, cols, target):
    r = lax.broadcasted_iota(jnp.int32, (rows, cols), 0)
    q = lax.broadcasted_iota(jnp.int32, (rows, cols), 1)
    return jnp.where(target(r, q), 1.0, 0.0).astype(BF16)


def lane_shift(x, s):
    if s == 0:
        return x
    n = x.shape[1]
    z = lax.broadcasted_iota(jnp.int32, x.shape, 1)
    if s == 1:
        return jnp.where(z < n - 1, pltpu.roll(x, n - 1, 1), 0.0)
    return jnp.where(z > 0, pltpu.roll(x, 1, 1), 0.0)


def spread(out_ref, rows_of, cb, ys, zs):
    for y in range(ys):
        row = rows_of(y)
        for c in (-1, 0, 1):
            moved = lane_shift(row, -c)
            for b in (-1, 0, 1):
                j = 3 * (b + 1) + (c + 1)
                if 0 <= y + b < ys:
                    out_ref[j * cb : (j + 1) * cb, (y + b) * zs : (y + b + 1) * zs] = moved
    edge = jnp.zeros((3 * cb, zs), F32)
    out_ref[0 : 3 * cb, (ys - 1) * zs : ys * zs] = edge
    out_ref[6 * cb : 9 * cb, 0:zs] = edge


def kernel(
    n, nz, cb, ys, zs, scale, sp, ch_name,
    f_hbm, g_hbm, mask_hbm, w1_hbm, w2_hbm,
    gf_ref, g1_ref, g2_ref,
    w1_ref, w2_ref, mi_ref, ws, B, MK, MX, X, WA, WB, WCF, WC, TR, AC, SL, GPF, GP, SH, SM, TA, PA, PR,
    R32, PK, RB, RP, CS, GF,
    zss, zrs, hss, hrs, mss, mrs, mhs, mhr, pss, prs, r1s, r1r, r2s, r2r, r3s, r3r,
):
    s = lax.axis_index(sp)
    me = lax.axis_index(ch_name)
    full = w1_ref.shape[1]
    cells = ys * zs
    kb = X.shape[2]
    kc = GP.shape[0]
    cp = -(-cb // 16) * 16
    mz = mi_ref.shape[1]
    rows = 27 * cb
    main, rest = 21 * cb, 6 * cb
    half = RB.shape[2]
    ry = max(1, 256 // zs)
    nch = n // 2
    tiles = zs // 128
    core = lax.rem(s, 2)
    chip = lax.div(s, 2)
    partner = s + 1 - 2 * core
    left, right = s > 0, s < n - 1

    def copy(src, dst, ssem, rsem, ds, dc):
        return pltpu.make_async_remote_copy(
            src_ref=src, dst_ref=dst, send_sem=ssem, recv_sem=rsem,
            device_id=(ds, dc), device_id_type=MESH,
        )

    load_m = pltpu.make_async_copy(mask_hbm, mi_ref, ws.at[2])
    load_f = pltpu.make_async_copy(f_hbm, B.at[0, 1, me], ws.at[3])
    load_g = pltpu.make_async_copy(g_hbm, B.at[1, 1, me], ws.at[4])
    load1 = pltpu.make_async_copy(w1_hbm, w1_ref, ws.at[0])
    load2 = pltpu.make_async_copy(w2_hbm, w2_ref, ws.at[1])
    load_m.start()
    load_f.start()
    load_g.start()
    load1.start()
    load2.start()
    barrier = pltpu.get_barrier_semaphore()

    @pl.loop(1, nz)
    def _(i):
        pl.semaphore_signal(barrier, inc=1, device_id=(s, lax.rem(me + i, nz)), device_id_type=MESH)

    @pl.loop(1, n)
    def _(i):
        pl.semaphore_signal(barrier, inc=1, device_id=(lax.rem(s + i, n), me), device_id_type=MESH)

    load_m.wait()
    place = one_hot(mz, zs, lambda r, q: q == r + mz * me)
    MK[me] = dot_nn(mi_ref[...].astype(F32).astype(BF16), place)
    load_f.wait()
    load_g.wait()
    pl.semaphore_wait(barrier, n + nz - 2)

    def z_copy(i, buf, ssem, rsem):
        return copy(buf, buf, ssem.at[i], rsem.at[i], s, lax.rem(me + i, nz))

    order = sorted(range(1, nz), key=lambda i: min(i, nz - i))
    for i in order:
        z_copy(i, MK.at[me], mss, mrs).start()
    for kind in range(2):
        for to in range(nz):

            @pl.when(me != to)
            def _():
                z_copy(lax.rem(to - me + nz, nz), B.at[kind, 1, me], zss.at[kind], zrs.at[kind]).start()

    def halo(kind, c, start):
        src = B.at[kind, 1, c]

        @pl.when(right)
        def _():
            d = copy(src, B.at[kind, 0, c], hss.at[kind, 0, c], hrs.at[kind, 0, c], s + 1, me)
            d.start() if start else d.wait_send()

        @pl.when(left)
        def _():
            d = copy(src, B.at[kind, 2, c], hss.at[kind, 1, c], hrs.at[kind, 1, c], s - 1, me)
            d.start() if start else d.wait_send()

    halo(1, me, True)
    halo(0, me, True)

    for kind in range(2):
        X[kind] = jnp.zeros(X.shape[1:], BF16)
    GP[...] = jnp.zeros(GP.shape, BF16)
    WCF[...] = jnp.zeros(WCF.shape, F32)
    PK[...] = jnp.zeros(PK.shape, F32)
    load1.wait()
    load2.wait()
    pick = one_hot(cb, full, lambda r, q: q == r + cb * me)
    same = one_hot(full, full, lambda r, q: q == r)
    widen = one_hot(kb, full, lambda r, q: r == (q // cb) * cp + lax.rem(q, cb))
    for a in range(3):
        for b in range(3):
            lanes = slice((3 * a + b) * kb, (3 * a + b + 1) * kb)
            for c in range(3):
                k = 9 * a + 3 * b + c
                w1 = w1_ref[k]
                wide = dot_nn(widen, w1).astype(BF16)
                WA[c * full : (c + 1) * full, lanes] = dot_nt(same, wide).astype(BF16)
                WB[c * full : (c + 1) * full, lanes] = dot_nt(w2_ref[k], widen).astype(BF16)
                WCF[(3 * a + c) * cb : (3 * a + c + 1) * cb, b * kc : b * kc + full] = dot_nn(pick, w1)
    WC[...] = WCF[...].astype(BF16)

    for i in order:
        c = lax.rem(me + nz - i, nz)
        copy(MK.at[c], MK.at[c], mss.at[i], mrs.at[i], s, c).wait_recv()
    own_mask = MK[0]
    for c in range(1, nz):
        own_mask = own_mask + MK[c]
    MX[1] = own_mask

    @pl.when(right)
    def _():
        copy(MX.at[1], MX.at[0], mhs.at[0], mhr.at[0], s + 1, me).start()

    @pl.when(left)
    def _():
        copy(MX.at[1], MX.at[2], mhs.at[1], mhr.at[1], s - 1, me).start()

    def native(kind, slab, c):
        x = B[kind, slab, c].astype(F32)
        if kind:
            x = (x.reshape(cb, ys, zs) * MX[slab][None]).reshape(cb * ys, zs)
        return x

    def put(ref, x):
        for q in range(tiles):
            ref[q] = x[:, q * 128 : (q + 1) * 128]

    def take(ref, y):
        return jnp.concatenate([ref[q, pl.ds(y, cb, stride=ys), :] for q in range(tiles)], axis=1)

    def whole(ref):
        return jnp.concatenate([ref[q] for q in range(tiles)], axis=1)

    def relayout(kind, slab, c, t):
        put(TR.at[t], native(kind, slab, c))
        at = pl.ds(pl.multiple_of(c * cp, 16), cb)
        for y in range(ys):
            X[kind, slab, at, (1 + y) * zs : (2 + y) * zs] = take(TR.at[t], y).astype(BF16)

    def arrive(kind):
        for i in order:
            c = lax.rem(me + nz - i, nz)
            copy(B.at[kind, 1, c], B.at[kind, 1, c], zss.at[kind, i], zrs.at[kind, i], s, c).wait_recv()
            halo(kind, c, True)
            relayout(kind, 1, c, i)

    def arrive_halo(kind):
        for side, slab, there in ((0, 0, left), (1, 2, right)):

            @pl.when(there)
            def _():
                for c in range(nz):
                    copy(B.at[kind, slab, c], B.at[kind, slab, c], hss.at[kind, side, c], hrs.at[kind, side, c], s, me).wait_recv()
                    relayout(kind, slab, c, c)

    def conv(kind, W, step, direction):
        for y0 in range(0, ys, ry):
            parts = []
            for a in range(3):
                slab = a if direction == 1 else 2 - a
                for b in range(3):
                    y = y0 + 1 + direction * (b - 1)
                    parts.append(X[kind, slab, :, y * zs : (y + ry) * zs])
            res = dot_nn(W[...], jnp.concatenate(parts, axis=0))
            for r in range(ry):
                acc = None
                for c in range(3):
                    piece = lane_shift(res[c * full : (c + 1) * full, r * zs : (r + 1) * zs], direction * (c - 1))
                    acc = piece if acc is None else acc + piece
                step(y0 + r, acc)

    relayout(0, 1, me, 0)
    arrive(0)
    def spread_masked(slab):
        put(TR.at[0], native(1, slab, me))
        spread(SH, lambda y: take(TR.at[0], y), cb, ys, zs)
        SM[2 - slab] = SH[...].astype(BF16)

    spread_masked(1)
    for side, slab, there in ((0, 0, left), (1, 2, right)):

        @pl.when(there)
        def _():
            copy(MX.at[slab], MX.at[slab], mhs.at[side], mhr.at[side], s, me).wait_recv()
            copy(B.at[1, slab, me], B.at[1, slab, me], hss.at[1, side, me], hrs.at[1, side, me], s, me).wait_recv()
            spread_masked(slab)

        @pl.when(jnp.logical_not(there))
        def _():
            SM[2 - slab] = jnp.zeros(SM.shape[1:], BF16)

    relayout(1, 1, me, 0)
    arrive(1)

    arrive_halo(0)

    def pre_step(y, acc):
        at = slice(y * zs, (y + 1) * zs)
        m = MX[1, y : y + 1, :]
        pre = acc * m
        sig = jax.nn.sigmoid(pre)
        AC[:, at] = (pre * sig).astype(BF16)
        SL[:, at] = sig * (1.0 + pre * (1.0 - sig)) * m

    conv(0, WA, pre_step, 1)

    def pair_start(g):
        PK[g, 0:main, 0:full] = R32[g, 0:main, :]
        for p in range(3):
            PK[g, p * rest : (p + 1) * rest, full:128] = R32[g, main:rows, 32 * p : 32 * p + 32]
        RB[g] = PK[g].astype(BF16).reshape(RB.shape[1:])
        copy(RB.at[g, 1 - core], RP.at[g], r1s.at[g], r1r.at[g], partner, me).start()

    def chips(g, start):
        @pl.loop(1, nch)
        def _(i):
            to = lax.rem(chip + i, nch)
            d = copy(CS.at[g, chip], CS.at[g, chip], r2s.at[g, i], r2r.at[g, i], 2 * to + core, me)
            d.start() if start else d.wait_send()

    def chip_sum(g):
        copy(RP.at[g], RP.at[g], r1s.at[g], r1r.at[g], partner, me).wait_recv()
        mine = PK[g, pl.ds(pl.multiple_of(core * half, 8), half), :]
        CS[g, chip] = (mine + RP[g].astype(F32)).astype(BF16)
        chips(g, True)

    def total(g):
        @pl.loop(1, nch)
        def _(i):
            j = lax.rem(chip + nch - i, nch)
            copy(CS.at[g, j], CS.at[g, j], r2s.at[g, i], r2r.at[g, i], s, me).wait_recv()

        acc = CS[g, 0].astype(F32)
        for j in range(1, nch):
            acc = acc + CS[g, j].astype(F32)
        GF[g, core] = acc
        copy(GF.at[g, core], GF.at[g, core], r3s.at[g], r3r.at[g], partner, me).start()

    def finish(g, out_ref):
        other = GF.at[g, 1 - core]
        copy(other, other, r3s.at[g], r3r.at[g], partner, me).wait_recv()
        done = GF[g].reshape(PK.shape[1:])
        out_ref[0:main, :] = done[0:main, 0:full]
        for p in range(3):
            out_ref[main:rows, 32 * p : 32 * p + 32] = done[p * rest : (p + 1) * rest, full:128]

    for a in range(3):
        R32[1, 9 * cb * a : 9 * cb * (a + 1), :] = dot_nt(SM[a], AC[...]) * scale
    pair_start(1)

    def wait_halo_grads():
        for side, slab, there in ((0, 0, left), (1, 2, right)):

            @pl.when(there)
            def _():
                relayout(1, slab, me, 0)

                @pl.loop(1, nz)
                def _(i):
                    c = lax.rem(me + i, nz)
                    copy(B.at[1, slab, c], B.at[1, slab, c], hss.at[1, side, c], hrs.at[1, side, c], s, me).wait_recv()
                    relayout(1, slab, c, i)

    wait_halo_grads()
    chip_sum(1)

    def back_step(y, acc):
        gp = acc * SL[:, y * zs : (y + 1) * zs]
        GPF[:, y * zs : (y + 1) * zs] = gp
        GP[0:full, (1 + y) * zs : (2 + y) * zs] = gp.astype(BF16)

    conv(1, WB, back_step, -1)

    own_rows = pl.ds(pl.multiple_of(me * cb, 8), cb)
    spread(SH, lambda y: GPF[own_rows, y * zs : (y + 1) * zs], cb, ys, zs)
    moved = SH[...].astype(BF16)
    narrow = one_hot(full, kb, lambda r, q: q == (r // cb) * cp + lax.rem(r, cb))
    for a in range(3):
        wide = (dot_nt(moved, X[0, a, :, zs : zs + cells]) * scale).astype(BF16)
        R32[0, 9 * cb * a : 9 * cb * (a + 1), :] = dot_nt(wide, narrow)
    pair_start(0)

    for y0 in range(0, ys, ry):
        parts = []
        for b in range(3):
            y = y0 + 1 - (b - 1)
            parts.append(GP[:, y * zs : (y + ry) * zs])
        res = dot_nn(WC[...], jnp.concatenate(parts, axis=0))
        for a in range(3):
            for r in range(ry):
                acc = None
                for c in range(3):
                    j = 3 * a + c
                    piece = lane_shift(res[j * cb : (j + 1) * cb, r * zs : (r + 1) * zs], -(c - 1))
                    acc = piece if acc is None else acc + piece
                for q in range(tiles):
                    TA[a, q, pl.ds(y0 + r, cb, stride=ys), :] = acc[:, q * 128 : (q + 1) * 128]
    PA[0] = whole(TA.at[0]).astype(BF16)
    PA[1] = whole(TA.at[2]).astype(BF16)

    chip_sum(0)

    @pl.when(right)
    def _():
        copy(PA.at[1], PR.at[0], pss.at[0], prs.at[0], s + 1, me).start()

    @pl.when(left)
    def _():
        copy(PA.at[0], PR.at[1], pss.at[1], prs.at[1], s - 1, me).start()

    total(1)

    total(0)
    for side, there in ((0, left), (1, right)):

        @pl.when(there)
        def _():
            copy(PR.at[side], PR.at[side], pss.at[side], prs.at[side], s, me).wait_recv()
            put(TA.at[1], whole(TA.at[1]) + PR[side].astype(F32))

    gf = whole(TA.at[1]).reshape(cb, ys, zs) * MX[1][None]
    gf_ref[...] = gf.reshape(cb * ys, zs).astype(BF16)

    finish(1, g2_ref)
    finish(0, g1_ref)

    for i in order:
        z_copy(i, MK.at[me], mss, mrs).wait_send()
        for kind in range(2):
            z_copy(i, B.at[kind, 1, me], zss.at[kind], zrs.at[kind]).wait_send()

    @pl.when(right)
    def _():
        copy(MX.at[1], MX.at[0], mhs.at[0], mhr.at[0], s + 1, me).wait_send()
        copy(PA.at[1], PR.at[0], pss.at[0], prs.at[0], s + 1, me).wait_send()

    @pl.when(left)
    def _():
        copy(MX.at[1], MX.at[2], mhs.at[1], mhr.at[1], s - 1, me).wait_send()
        copy(PA.at[0], PR.at[1], pss.at[1], prs.at[1], s - 1, me).wait_send()

    @pl.loop(0, nz)
    def _(c):
        halo(0, c, False)
        halo(1, c, False)

    for g in range(2):
        copy(RB.at[g, 1 - core], RP.at[g], r1s.at[g], r1r.at[g], partner, me).wait_send()
        chips(g, False)
        copy(GF.at[g, core], GF.at[g, core], r3s.at[g], r3r.at[g], partner, me).wait_send()


def store(gf_ref, g1_ref, g2_ref, gf_hbm, g1_hbm, g2_hbm, sems):
    copies = [
        pltpu.make_async_copy(g1_ref, g1_hbm, sems.at[0]),
        pltpu.make_async_copy(g2_ref, g2_hbm, sems.at[1]),
        pltpu.make_async_copy(gf_ref, gf_hbm, sems.at[2]),
    ]
    for c in copies:
        c.start()
    for c in copies:
        c.wait()


def up(value, step):
    return -(-value // step) * step


def body(n, nz, feats, grads, mask, w_first, w_second):
    cb, _, ys, zs = feats.shape
    taps, full, _ = w_first.shape
    cells = ys * zs
    ex = (ys + 2) * zs
    mz = mask.shape[2]
    scale = float((n * ys * zs) ** -0.5)
    rows = taps * cb
    half = up(-(-21 * cb // 2), 16)
    cp = up(cb, 16)
    kb = up(nz * cp, 128)
    kc = up(full, 128)
    vm = pltpu.VMEM
    dma = pltpu.SemaphoreType.DMA
    spec = pl.BlockSpec(memory_space=pltpu.VMEM)
    hbm = pl.BlockSpec(memory_space=pltpu.HBM)
    flat = (cb * ys, zs)
    split = (zs // 128, cb * ys, 128)
    gf, g1, g2 = pl.pallas_call(
        functools.partial(kernel, n, nz, cb, ys, zs, scale, "space", "chan"),
        out_shape=(
            jax.ShapeDtypeStruct(flat, BF16),
            jax.ShapeDtypeStruct((rows, full), F32),
            jax.ShapeDtypeStruct((rows, full), F32),
        ),
        in_specs=[hbm] * 5,
        out_specs=(spec,) * 3,
        scratch_shapes=[
            vm((taps, full, full), BF16), vm((taps, full, full), BF16), vm((ys, mz), jnp.int32), dma((5,)),
            vm((2, 3, nz, *flat), BF16),
            vm((nz, ys, zs), F32),
            vm((3, ys, zs), F32),
            vm((2, 3, kb, ex), BF16),
            vm((3 * full, 9 * kb), BF16),
            vm((3 * full, 9 * kb), BF16),
            vm((9 * cb, 3 * kc), F32),
            vm((9 * cb, 3 * kc), BF16),
            vm((nz + 1, *split), F32),
            vm((full, cells), BF16),
            vm((full, cells), F32),
            vm((full, cells), F32),
            vm((kc, ex), BF16),
            vm((9 * cb, cells), F32),
            vm((3, 9 * cb, cells), BF16),
            vm((3, *split), F32),
            vm((2, *flat), BF16),
            vm((2, *flat), BF16),
            vm((2, rows, full), F32),
            vm((2, 2 * half, 128), F32),
            vm((2, 2, half, 128), BF16),
            vm((2, half, 128), BF16),
            vm((2, n // 2, half, 128), BF16),
            vm((2, 2, half, 128), F32),
            dma((2, nz)), dma((2, nz)), dma((2, 2, nz)), dma((2, 2, nz)),
            dma((nz,)), dma((nz,)), dma((2,)), dma((2,)), dma((2,)), dma((2,)),
            dma((2,)), dma((2,)), dma((2, n // 2)), dma((2, n // 2)), dma((2,)), dma((2,)),
        ],
        compiler_params=pltpu.CompilerParams(
            collective_id=0, has_side_effects=True, vmem_limit_bytes=48 << 20
        ),
    )(*(pltpu.with_memory_space_constraint(x, pltpu.HBM) for x in (
        feats.reshape(flat), grads.reshape(flat), mask.reshape(ys, mz), w_first, w_second)))
    gf, g1, g2 = pl.pallas_call(
        store,
        out_shape=(
            jax.ShapeDtypeStruct(flat, BF16),
            jax.ShapeDtypeStruct((rows, full), F32),
            jax.ShapeDtypeStruct((rows, full), F32),
        ),
        in_specs=[spec] * 3,
        out_specs=(hbm,) * 3,
        scratch_shapes=[dma((3,))],
    )(*(pltpu.with_memory_space_constraint(x, pltpu.VMEM) for x in (gf, g1, g2)))
    return (
        gf.reshape(cb, 1, ys, zs),
        g1.reshape(taps, cb, full).transpose(0, 2, 1),
        g2.reshape(taps, cb, full).transpose(0, 2, 1),
    )


def solution(mesh):
    in_specs = (
        P("chan", "space", None, None),
        P("chan", "space", None, None),
        P("space", None, "chan"),
        P(),
        P(),
    )
    out_specs = (P("chan", "space", None, None), P(None, None, "chan"), P(None, None, "chan"))
    sizes = (mesh.shape["space"], mesh.shape["chan"])
    return jax.shard_map(
        functools.partial(body, *sizes),
        mesh=mesh, in_specs=in_specs, out_specs=out_specs, check_vma=False,
    )
```

```python
import functools

import jax
import jax.numpy as jnp
from jax import lax
from jax.experimental import pallas as pl
from jax.experimental.pallas import tpu as pltpu
from jax.sharding import PartitionSpec as P

MESH = pl.DeviceIdType.MESH
F32 = jnp.float32
BF16 = jnp.bfloat16


def dot_nn(left, right):
    return jnp.dot(left, right, preferred_element_type=F32)


def dot_nt(left, right):
    return lax.dot_general(left, right, (((1,), (1,)), ((), ())), preferred_element_type=F32)


def one_hot(rows, cols, target):
    r = lax.broadcasted_iota(jnp.int32, (rows, cols), 0)
    q = lax.broadcasted_iota(jnp.int32, (rows, cols), 1)
    return jnp.where(target(r, q), 1.0, 0.0).astype(BF16)


def lane_shift(x, s):
    if s == 0:
        return x
    n = x.shape[1]
    z = lax.broadcasted_iota(jnp.int32, x.shape, 1)
    if s == 1:
        return jnp.where(z < n - 1, pltpu.roll(x, n - 1, 1), 0.0)
    return jnp.where(z > 0, pltpu.roll(x, 1, 1), 0.0)


def spread(out_ref, rows_of, cb, ys, zs):
    for y in range(ys):
        row = rows_of(y)
        for c in (-1, 0, 1):
            moved = lane_shift(row, -c)
            for b in (-1, 0, 1):
                j = 3 * (b + 1) + (c + 1)
                if 0 <= y + b < ys:
                    out_ref[j * cb : (j + 1) * cb, (y + b) * zs : (y + b + 1) * zs] = moved
    edge = jnp.zeros((3 * cb, zs), F32)
    out_ref[0 : 3 * cb, (ys - 1) * zs : ys * zs] = edge
    out_ref[6 * cb : 9 * cb, 0:zs] = edge


def kernel(
    n, nz, cb, ys, zs, scale, sp, ch_name,
    f_hbm, g_hbm, mask_hbm, w1_hbm, w2_hbm,
    gf_ref, g1_ref, g2_ref,
    w1_ref, w2_ref, mi_ref, ws, B, MK, MX, X, WA, WB, WCF, WC, TR, AC, SL, GPF, GP, SH, SM, TA, PA, PR,
    R32, PK, RB, RP, CS, GF,
    zss, zrs, hss, hrs, mss, mrs, mhs, mhr, pss, prs, r1s, r1r, r2s, r2r, r3s, r3r,
):
    s = lax.axis_index(sp)
    me = lax.axis_index(ch_name)
    full = w1_ref.shape[1]
    cells = ys * zs
    kb = X.shape[2]
    kc = GP.shape[0]
    cp = -(-cb // 16) * 16
    mz = mi_ref.shape[1]
    rows = 27 * cb
    main, rest = 21 * cb, 6 * cb
    half = RB.shape[2]
    ry = max(1, 256 // zs)
    nch = n // 2
    tiles = zs // 128
    core = lax.rem(s, 2)
    chip = lax.div(s, 2)
    partner = s + 1 - 2 * core
    left, right = s > 0, s < n - 1

    def copy(src, dst, ssem, rsem, ds, dc):
        return pltpu.make_async_remote_copy(
            src_ref=src, dst_ref=dst, send_sem=ssem, recv_sem=rsem,
            device_id=(ds, dc), device_id_type=MESH,
        )

    load_m = pltpu.make_async_copy(mask_hbm, mi_ref, ws.at[2])
    load_f = pltpu.make_async_copy(f_hbm, B.at[0, 1, me], ws.at[3])
    load_g = pltpu.make_async_copy(g_hbm, B.at[1, 1, me], ws.at[4])
    load1 = pltpu.make_async_copy(w1_hbm, w1_ref, ws.at[0])
    load2 = pltpu.make_async_copy(w2_hbm, w2_ref, ws.at[1])
    load_m.start()
    load_f.start()
    load_g.start()
    load1.start()
    load2.start()
    barrier = pltpu.get_barrier_semaphore()

    @pl.loop(1, nz)
    def _(i):
        pl.semaphore_signal(barrier, inc=1, device_id=(s, lax.rem(me + i, nz)), device_id_type=MESH)

    @pl.loop(1, n)
    def _(i):
        pl.semaphore_signal(barrier, inc=1, device_id=(lax.rem(s + i, n), me), device_id_type=MESH)

    load_m.wait()
    place = one_hot(mz, zs, lambda r, q: q == r + mz * me)
    MK[me] = dot_nn(mi_ref[...].astype(F32).astype(BF16), place)
    load_f.wait()
    load_g.wait()
    pl.semaphore_wait(barrier, n + nz - 2)

    def z_copy(i, buf, ssem, rsem):
        return copy(buf, buf, ssem.at[i], rsem.at[i], s, lax.rem(me + i, nz))

    order = sorted(range(1, nz), key=lambda i: min(i, nz - i))
    for i in order:
        z_copy(i, MK.at[me], mss, mrs).start()
    for kind in range(2):
        for to in range(nz):

            @pl.when(me != to)
            def _():
                z_copy(lax.rem(to - me + nz, nz), B.at[kind, 1, me], zss.at[kind], zrs.at[kind]).start()

    def halo(kind, c, start):
        src = B.at[kind, 1, c]

        @pl.when(right)
        def _():
            d = copy(src, B.at[kind, 0, c], hss.at[kind, 0, c], hrs.at[kind, 0, c], s + 1, me)
            d.start() if start else d.wait_send()

        @pl.when(left)
        def _():
            d = copy(src, B.at[kind, 2, c], hss.at[kind, 1, c], hrs.at[kind, 1, c], s - 1, me)
            d.start() if start else d.wait_send()

    halo(1, me, True)
    halo(0, me, True)

    for kind in range(2):
        X[kind] = jnp.zeros(X.shape[1:], BF16)
    GP[...] = jnp.zeros(GP.shape, BF16)
    WCF[...] = jnp.zeros(WCF.shape, F32)
    PK[...] = jnp.zeros(PK.shape, F32)
    load1.wait()
    load2.wait()
    pick = one_hot(cb, full, lambda r, q: q == r + cb * me)
    same = one_hot(full, full, lambda r, q: q == r)
    widen = one_hot(kb, full, lambda r, q: r == (q // cb) * cp + lax.rem(q, cb))
    for a in range(3):
        for b in range(3):
            lanes = slice((3 * a + b) * kb, (3 * a + b + 1) * kb)
            for c in range(3):
                k = 9 * a + 3 * b + c
                w1 = w1_ref[k]
                wide = dot_nn(widen, w1).astype(BF16)
                WA[c * full : (c + 1) * full, lanes] = dot_nt(same, wide).astype(BF16)
                WB[c * full : (c + 1) * full, lanes] = dot_nt(w2_ref[k], widen).astype(BF16)
                WCF[(3 * a + c) * cb : (3 * a + c + 1) * cb, b * kc : b * kc + full] = dot_nn(pick, w1)
    WC[...] = WCF[...].astype(BF16)

    for i in order:
        c = lax.rem(me + nz - i, nz)
        copy(MK.at[c], MK.at[c], mss.at[i], mrs.at[i], s, c).wait_recv()
    own_mask = MK[0]
    for c in range(1, nz):
        own_mask = own_mask + MK[c]
    MX[1] = own_mask

    @pl.when(right)
    def _():
        copy(MX.at[1], MX.at[0], mhs.at[0], mhr.at[0], s + 1, me).start()

    @pl.when(left)
    def _():
        copy(MX.at[1], MX.at[2], mhs.at[1], mhr.at[1], s - 1, me).start()

    def native(kind, slab, c):
        x = B[kind, slab, c].astype(F32)
        if kind:
            x = (x.reshape(cb, ys, zs) * MX[slab][None]).reshape(cb * ys, zs)
        return x

    def put(ref, x):
        for q in range(tiles):
            ref[q] = x[:, q * 128 : (q + 1) * 128]

    def take(ref, y):
        return jnp.concatenate([ref[q, pl.ds(y, cb, stride=ys), :] for q in range(tiles)], axis=1)

    def whole(ref):
        return jnp.concatenate([ref[q] for q in range(tiles)], axis=1)

    def relayout(kind, slab, c, t):
        put(TR.at[t], native(kind, slab, c))
        at = pl.ds(pl.multiple_of(c * cp, 16), cb)
        for y in range(ys):
            X[kind, slab, at, (1 + y) * zs : (2 + y) * zs] = take(TR.at[t], y).astype(BF16)

    def arrive(kind):
        for i in order:
            c = lax.rem(me + nz - i, nz)
            copy(B.at[kind, 1, c], B.at[kind, 1, c], zss.at[kind, i], zrs.at[kind, i], s, c).wait_recv()
            halo(kind, c, True)
            relayout(kind, 1, c, i)

    def arrive_halo(kind):
        for side, slab, there in ((0, 0, left), (1, 2, right)):

            @pl.when(there)
            def _():
                for c in range(nz):
                    copy(B.at[kind, slab, c], B.at[kind, slab, c], hss.at[kind, side, c], hrs.at[kind, side, c], s, me).wait_recv()
                    relayout(kind, slab, c, c)

    def conv(kind, W, step, direction):
        for y0 in range(0, ys, ry):
            parts = []
            for a in range(3):
                slab = a if direction == 1 else 2 - a
                for b in range(3):
                    y = y0 + 1 + direction * (b - 1)
                    parts.append(X[kind, slab, :, y * zs : (y + ry) * zs])
            res = dot_nn(W[...], jnp.concatenate(parts, axis=0))
            for r in range(ry):
                acc = None
                for c in range(3):
                    piece = lane_shift(res[c * full : (c + 1) * full, r * zs : (r + 1) * zs], direction * (c - 1))
                    acc = piece if acc is None else acc + piece
                step(y0 + r, acc)

    relayout(0, 1, me, 0)
    arrive(0)
    def spread_masked(slab):
        put(TR.at[0], native(1, slab, me))
        spread(SH, lambda y: take(TR.at[0], y), cb, ys, zs)
        SM[2 - slab] = SH[...].astype(BF16)

    spread_masked(1)
    for side, slab, there in ((0, 0, left), (1, 2, right)):

        @pl.when(there)
        def _():
            copy(MX.at[slab], MX.at[slab], mhs.at[side], mhr.at[side], s, me).wait_recv()
            copy(B.at[1, slab, me], B.at[1, slab, me], hss.at[1, side, me], hrs.at[1, side, me], s, me).wait_recv()
            spread_masked(slab)

        @pl.when(jnp.logical_not(there))
        def _():
            SM[2 - slab] = jnp.zeros(SM.shape[1:], BF16)

    relayout(1, 1, me, 0)
    arrive(1)

    arrive_halo(0)

    def pre_step(y, acc):
        at = slice(y * zs, (y + 1) * zs)
        m = MX[1, y : y + 1, :]
        pre = acc * m
        sig = jax.nn.sigmoid(pre)
        AC[:, at] = (pre * sig).astype(BF16)
        SL[:, at] = sig * (1.0 + pre * (1.0 - sig)) * m

    conv(0, WA, pre_step, 1)

    def pair_start(g):
        PK[g, 0:main, 0:full] = R32[g, 0:main, :]
        for p in range(3):
            PK[g, p * rest : (p + 1) * rest, full:128] = R32[g, main:rows, 32 * p : 32 * p + 32]
        RB[g] = PK[g].astype(BF16).reshape(RB.shape[1:])
        copy(RB.at[g, 1 - core], RP.at[g], r1s.at[g], r1r.at[g], partner, me).start()

    def chips(g, start):
        @pl.loop(1, nch)
        def _(i):
            to = lax.rem(chip + i, nch)
            d = copy(CS.at[g, chip], CS.at[g, chip], r2s.at[g, i], r2r.at[g, i], 2 * to + core, me)
            d.start() if start else d.wait_send()

    def chip_sum(g):
        copy(RP.at[g], RP.at[g], r1s.at[g], r1r.at[g], partner, me).wait_recv()
        mine = PK[g, pl.ds(pl.multiple_of(core * half, 8), half), :]
        CS[g, chip] = (mine + RP[g].astype(F32)).astype(BF16)
        chips(g, True)

    def total(g):
        @pl.loop(1, nch)
        def _(i):
            j = lax.rem(chip + nch - i, nch)
            copy(CS.at[g, j], CS.at[g, j], r2s.at[g, i], r2r.at[g, i], s, me).wait_recv()

        acc = CS[g, 0].astype(F32)
        for j in range(1, nch):
            acc = acc + CS[g, j].astype(F32)
        GF[g, core] = acc
        copy(GF.at[g, core], GF.at[g, core], r3s.at[g], r3r.at[g], partner, me).start()

    def finish(g, out_ref):
        other = GF.at[g, 1 - core]
        copy(other, other, r3s.at[g], r3r.at[g], partner, me).wait_recv()
        done = GF[g].reshape(PK.shape[1:])
        out_ref[0:main, :] = done[0:main, 0:full]
        for p in range(3):
            out_ref[main:rows, 32 * p : 32 * p + 32] = done[p * rest : (p + 1) * rest, full:128]

    for a in range(3):
        R32[1, 9 * cb * a : 9 * cb * (a + 1), :] = dot_nt(SM[a], AC[...]) * scale
    pair_start(1)

    def wait_halo_grads():
        for side, slab, there in ((0, 0, left), (1, 2, right)):

            @pl.when(there)
            def _():
                relayout(1, slab, me, 0)

                @pl.loop(1, nz)
                def _(i):
                    c = lax.rem(me + i, nz)
                    copy(B.at[1, slab, c], B.at[1, slab, c], hss.at[1, side, c], hrs.at[1, side, c], s, me).wait_recv()
                    relayout(1, slab, c, i)

    wait_halo_grads()
    chip_sum(1)

    def back_step(y, acc):
        gp = acc * SL[:, y * zs : (y + 1) * zs]
        GPF[:, y * zs : (y + 1) * zs] = gp
        GP[0:full, (1 + y) * zs : (2 + y) * zs] = gp.astype(BF16)

    conv(1, WB, back_step, -1)

    own_rows = pl.ds(pl.multiple_of(me * cb, 8), cb)
    spread(SH, lambda y: GPF[own_rows, y * zs : (y + 1) * zs], cb, ys, zs)
    moved = SH[...].astype(BF16)
    narrow = one_hot(full, kb, lambda r, q: q == (r // cb) * cp + lax.rem(r, cb))
    for a in range(3):
        wide = (dot_nt(moved, X[0, a, :, zs : zs + cells]) * scale).astype(BF16)
        R32[0, 9 * cb * a : 9 * cb * (a + 1), :] = dot_nt(wide, narrow)
    pair_start(0)

    for y0 in range(0, ys, ry):
        if y0 == ys // 2:
            chip_sum(0)
        parts = []
        for b in range(3):
            y = y0 + 1 - (b - 1)
            parts.append(GP[:, y * zs : (y + ry) * zs])
        res = dot_nn(WC[...], jnp.concatenate(parts, axis=0))
        for a in range(3):
            for r in range(ry):
                acc = None
                for c in range(3):
                    j = 3 * a + c
                    piece = lane_shift(res[j * cb : (j + 1) * cb, r * zs : (r + 1) * zs], -(c - 1))
                    acc = piece if acc is None else acc + piece
                for q in range(tiles):
                    TA[a, q, pl.ds(y0 + r, cb, stride=ys), :] = acc[:, q * 128 : (q + 1) * 128]
    PA[0] = whole(TA.at[0]).astype(BF16)
    PA[1] = whole(TA.at[2]).astype(BF16)

    @pl.when(right)
    def _():
        copy(PA.at[1], PR.at[0], pss.at[0], prs.at[0], s + 1, me).start()

    @pl.when(left)
    def _():
        copy(PA.at[0], PR.at[1], pss.at[1], prs.at[1], s - 1, me).start()

    total(1)

    total(0)
    for side, there in ((0, left), (1, right)):

        @pl.when(there)
        def _():
            copy(PR.at[side], PR.at[side], pss.at[side], prs.at[side], s, me).wait_recv()
            put(TA.at[1], whole(TA.at[1]) + PR[side].astype(F32))

    gf = whole(TA.at[1]).reshape(cb, ys, zs) * MX[1][None]
    gf_ref[...] = gf.reshape(cb * ys, zs).astype(BF16)

    finish(1, g2_ref)
    finish(0, g1_ref)

    for i in order:
        z_copy(i, MK.at[me], mss, mrs).wait_send()
        for kind in range(2):
            z_copy(i, B.at[kind, 1, me], zss.at[kind], zrs.at[kind]).wait_send()

    @pl.when(right)
    def _():
        copy(MX.at[1], MX.at[0], mhs.at[0], mhr.at[0], s + 1, me).wait_send()
        copy(PA.at[1], PR.at[0], pss.at[0], prs.at[0], s + 1, me).wait_send()

    @pl.when(left)
    def _():
        copy(MX.at[1], MX.at[2], mhs.at[1], mhr.at[1], s - 1, me).wait_send()
        copy(PA.at[0], PR.at[1], pss.at[1], prs.at[1], s - 1, me).wait_send()

    @pl.loop(0, nz)
    def _(c):
        halo(0, c, False)
        halo(1, c, False)

    for g in range(2):
        copy(RB.at[g, 1 - core], RP.at[g], r1s.at[g], r1r.at[g], partner, me).wait_send()
        chips(g, False)
        copy(GF.at[g, core], GF.at[g, core], r3s.at[g], r3r.at[g], partner, me).wait_send()


def store(gf_ref, g1_ref, g2_ref, gf_hbm, g1_hbm, g2_hbm, sems):
    copies = [
        pltpu.make_async_copy(g1_ref, g1_hbm, sems.at[0]),
        pltpu.make_async_copy(g2_ref, g2_hbm, sems.at[1]),
        pltpu.make_async_copy(gf_ref, gf_hbm, sems.at[2]),
    ]
    for c in copies:
        c.start()
    for c in copies:
        c.wait()


def up(value, step):
    return -(-value // step) * step


def body(n, nz, feats, grads, mask, w_first, w_second):
    cb, _, ys, zs = feats.shape
    taps, full, _ = w_first.shape
    cells = ys * zs
    ex = (ys + 2) * zs
    mz = mask.shape[2]
    scale = float((n * ys * zs) ** -0.5)
    rows = taps * cb
    half = up(-(-21 * cb // 2), 16)
    cp = up(cb, 16)
    kb = up(nz * cp, 128)
    kc = up(full, 128)
    vm = pltpu.VMEM
    dma = pltpu.SemaphoreType.DMA
    spec = pl.BlockSpec(memory_space=pltpu.VMEM)
    hbm = pl.BlockSpec(memory_space=pltpu.HBM)
    flat = (cb * ys, zs)
    split = (zs // 128, cb * ys, 128)
    gf, g1, g2 = pl.pallas_call(
        functools.partial(kernel, n, nz, cb, ys, zs, scale, "space", "chan"),
        out_shape=(
            jax.ShapeDtypeStruct(flat, BF16),
            jax.ShapeDtypeStruct((rows, full), F32),
            jax.ShapeDtypeStruct((rows, full), F32),
        ),
        in_specs=[hbm] * 5,
        out_specs=(spec,) * 3,
        scratch_shapes=[
            vm((taps, full, full), BF16), vm((taps, full, full), BF16), vm((ys, mz), jnp.int32), dma((5,)),
            vm((2, 3, nz, *flat), BF16),
            vm((nz, ys, zs), F32),
            vm((3, ys, zs), F32),
            vm((2, 3, kb, ex), BF16),
            vm((3 * full, 9 * kb), BF16),
            vm((3 * full, 9 * kb), BF16),
            vm((9 * cb, 3 * kc), F32),
            vm((9 * cb, 3 * kc), BF16),
            vm((nz + 1, *split), F32),
            vm((full, cells), BF16),
            vm((full, cells), F32),
            vm((full, cells), F32),
            vm((kc, ex), BF16),
            vm((9 * cb, cells), F32),
            vm((3, 9 * cb, cells), BF16),
            vm((3, *split), F32),
            vm((2, *flat), BF16),
            vm((2, *flat), BF16),
            vm((2, rows, full), F32),
            vm((2, 2 * half, 128), F32),
            vm((2, 2, half, 128), BF16),
            vm((2, half, 128), BF16),
            vm((2, n // 2, half, 128), BF16),
            vm((2, 2, half, 128), F32),
            dma((2, nz)), dma((2, nz)), dma((2, 2, nz)), dma((2, 2, nz)),
            dma((nz,)), dma((nz,)), dma((2,)), dma((2,)), dma((2,)), dma((2,)),
            dma((2,)), dma((2,)), dma((2, n // 2)), dma((2, n // 2)), dma((2,)), dma((2,)),
        ],
        compiler_params=pltpu.CompilerParams(
            collective_id=0, has_side_effects=True, vmem_limit_bytes=48 << 20
        ),
    )(*(pltpu.with_memory_space_constraint(x, pltpu.HBM) for x in (
        feats.reshape(flat), grads.reshape(flat), mask.reshape(ys, mz), w_first, w_second)))
    gf, g1, g2 = pl.pallas_call(
        store,
        out_shape=(
            jax.ShapeDtypeStruct(flat, BF16),
            jax.ShapeDtypeStruct((rows, full), F32),
            jax.ShapeDtypeStruct((rows, full), F32),
        ),
        in_specs=[spec] * 3,
        out_specs=(hbm,) * 3,
        scratch_shapes=[dma((3,))],
    )(*(pltpu.with_memory_space_constraint(x, pltpu.VMEM) for x in (gf, g1, g2)))
    return (
        gf.reshape(cb, 1, ys, zs),
        g1.reshape(taps, cb, full).transpose(0, 2, 1),
        g2.reshape(taps, cb, full).transpose(0, 2, 1),
    )


def solution(mesh):
    in_specs = (
        P("chan", "space", None, None),
        P("chan", "space", None, None),
        P("space", None, "chan"),
        P(),
        P(),
    )
    out_specs = (P("chan", "space", None, None), P(None, None, "chan"), P(None, None, "chan"))
    sizes = (mesh.shape["space"], mesh.shape["chan"])
    return jax.shard_map(
        functools.partial(body, *sizes),
        mesh=mesh, in_specs=in_specs, out_specs=out_specs, check_vma=False,
    )
```
